128 devices in a mesh: dp: 8 (over x, core), table: 16 (over y, z).
Axes of the slice: x: 4, y: 4, z: 4, core: 2. Of those that a mesh axis runs over, the one named last changes fastest.
Arguments:
- features: bfloat16 [16384, 2048], P(('dp', 'table')), may hold values from -6 to 6
- w_first: bfloat16 [2048, 1024], replicated, may hold values from -0.125 to 0.125
- b_first: float32 [1024], replicated, may hold values from -4 to 4
- grad_out: bfloat16 [16384, 1024], P(('dp', 'table')), may hold values from -6 to 6
- admit: int32 [16384, 16], P(('dp', 'table')), may hold values from 0 to 1, as said below
- owner: int32 [16384, 16, 1], P(('dp', 'table')), may hold values from 0 to 7, as said below
- adm_row: int32 [16384, 16], P(('dp', 'table')), may hold values from 0 to 2047
- q_shard: int32 [16384, 16, 1], P(('dp', 'table')), may hold values from 0 to 127, as said below
- q_local: int32 [16384, 16], P(('dp', 'table')), may hold values from 0 to 4095
- r_shard: int32 [16384, 16, 1], P(('dp', 'table')), may hold values from 0 to 127, as said below
- r_local: int32 [16384, 16], P(('dp', 'table')), may hold values from 0 to 4095
Outputs:
- w_grad: float32 [2048, 1024], replicated
- b_grad: float32 [1024], replicated
- adm_grad: float32 [16384, 128], P(('dp', 'table'))
- q_grad: float32 [524288, 128], P(('dp', 'table'))
- r_grad: float32 [524288, 128], P(('dp', 'table'))
The draws below stay inside these ranges and needn't reach their ends.
Inputs may be any that keep to these rules, and one draw needn't show every extreme that they name: `admit`: on some device every lookup is admitted, and on another device none is. Among the 2048 lookups of one device no owner is named more than 384 times, and on every device some owner exactly 384 times. `q_shard`: among the 2048 lookups of one device no block is named more than 24 times, and on every device some block exactly 24 times. `r_shard`: among the 2048 lookups of one device no block is named more than 24 times, and on every device some block exactly 24 times.
All inputs are finite; a program needn't handle non-finite values.
Results may differ from the reference program's by a relative error of at most 0.0055.
Values may be sent and summed in bfloat16 or wider, within the bound.
A program may use at most 128 MiB of HBM per device.

```python
import jax
import jax.numpy as jnp
from jax import lax

F = 16
E = 128
H = 1024
B_DEV = 128
QROWS_DEV = 4096
SAMPLES = 16384
ADM_ROWS = 16384
ADM_OWN = 2048
QROWS = 524288
CAP = 384
QCAP = 24
N_DP = 8
DEVICES = 128


def routed_labels(key, n_dest, most):
    count = B_DEV * F
    spare = count - most
    others = max(n_dest - 1, 1)
    base = spare // others
    reach = max(0, min((most - (spare + others - 1) // others) // 2, base // 2))

    def one_device(dev_key):
        key_one, key_two, key_cut, key_perm = jax.random.split(dev_key, 4)
        first = jax.random.randint(key_one, (), 0, n_dest)
        second = jax.random.randint(key_two, (), 0, n_dest)
        hottest = jnp.minimum(first, second).astype(jnp.int32)
        inner = jnp.arange(1, others, dtype=jnp.int32)
        jitter = jax.random.randint(key_cut, (others - 1,), -reach, reach + 1)
        cuts = (inner * spare // others + jitter).astype(jnp.int32)
        places = jnp.arange(count, dtype=jnp.int32)
        offset = places - most
        region = jnp.sum((offset[:, None] >= cuts[None, :]).astype(jnp.int32), axis=1)
        labels = jnp.where(places < most, hottest, (hottest + 1 + region) % n_dest).astype(jnp.int32)
        order = jax.random.permutation(key_perm, count)
        return labels[order]
    device_keys = jax.random.split(key, DEVICES)
    result = lax.map(one_device, device_keys)
    return result.reshape(SAMPLES, F, 1).astype(jnp.int32)


def draw_owner(key, part):
    return routed_labels(jax.random.fold_in(key, 11), N_DP, CAP)


def draw_q_shard(key, part):
    return routed_labels(jax.random.fold_in(key, 12), DEVICES, QCAP)


def draw_r_shard(key, part):
    return routed_labels(jax.random.fold_in(key, 13), DEVICES, QCAP)


def draw_admit(key, part):
    base_key = jax.random.fold_in(key, 14)
    key_full, key_empty, key_coin = jax.random.split(base_key, 3)
    full_dev = jax.random.randint(key_full, (), 0, DEVICES)
    empty_dev = (full_dev + 1 + jax.random.randint(key_empty, (), 0, DEVICES - 1)) % DEVICES
    coins = jax.random.randint(key_coin, (DEVICES, B_DEV * F), 0, 2)
    device_ids = jnp.arange(DEVICES, dtype=jnp.int32)[:, None]
    marks = jnp.where(device_ids == full_dev, 1, jnp.where(device_ids == empty_dev, 0, coins))
    return marks.reshape(SAMPLES, F).astype(jnp.int32)


def with_ends(entries, stream_key, low, top_value):
    index_at = [jax.random.randint(jax.random.fold_in(stream_key, axis), (), 0, length) for axis, length in enumerate(entries.shape)]
    widest = entries.shape.index(max(entries.shape))
    beside = index_at[:widest] + [(index_at[widest] + 1) % entries.shape[widest]] + index_at[widest + 1:]
    return entries.at[tuple(index_at)].set(low).at[tuple(beside)].set(top_value)


def levels(key, extent, shards, low, top_value):
    level, own = 1.0, jax.random.fold_in(key, 6)
    for dim, blocks in shards:
        steps = jnp.exp(jax.random.uniform(jax.random.fold_in(own, dim), (blocks,), jnp.float32, low / len(shards), top_value / len(shards)))
        level = level * jnp.repeat(steps, extent[dim] // blocks).reshape([-1 if axis == dim else 1 for axis in range(len(extent))])
    return level


def noise(key, shape, deviation, most, cuts=(), held_as=jnp.bfloat16):
    values = jax.random.normal(key, shape, jnp.float32) * deviation
    if len(cuts) > 0:
        values = levels(key, shape, cuts, -0.22, 0.18) * values
    return jnp.clip(values, min=-most, max=most).astype(held_as)


def setup_inputs(seed: int = 0) -> dict:
    streams_of = jax.random.split(jax.random.key(seed), 12)
    features = noise(streams_of[0], (SAMPLES, F * E), 1.0, 6.0, ((0, 128),))
    w_first = noise(streams_of[1], (F * E, H), (F * E) ** -0.5, 0.125)
    b_first = noise(streams_of[2], (H,), 1.0, 4.0, (), jnp.float32)
    grad_out = noise(streams_of[3], (SAMPLES, H), 1.0, 6.0, ((0, 128),))
    admit = draw_admit(jax.random.fold_in(streams_of[11], 71), 0)
    owner = draw_owner(jax.random.fold_in(streams_of[11], 71), 0)
    adm_row = with_ends(jax.random.randint(streams_of[6], (SAMPLES, F), 0, ADM_OWN), jax.random.fold_in(streams_of[6], 1), 0, ADM_OWN - 1).astype(jnp.int32)
    q_shard = draw_q_shard(jax.random.fold_in(streams_of[11], 71), 0)
    q_local = with_ends(jax.random.randint(streams_of[8], (SAMPLES, F), 0, QROWS_DEV), jax.random.fold_in(streams_of[8], 1), 0, QROWS_DEV - 1).astype(jnp.int32)
    r_shard = draw_r_shard(jax.random.fold_in(streams_of[11], 71), 0)
    r_local = with_ends(jax.random.randint(streams_of[10], (SAMPLES, F), 0, QROWS_DEV), jax.random.fold_in(streams_of[10], 1), 0, QROWS_DEV - 1).astype(jnp.int32)
    return {"features": features, "w_first": w_first, "b_first": b_first, "grad_out": grad_out, "admit": admit, "owner": owner, "adm_row": adm_row, "q_shard": q_shard, "q_local": q_local, "r_shard": r_shard, "r_local": r_local}


def reference(features, w_first, b_first, grad_out, admit, owner, adm_row, q_shard, q_local, r_shard, r_local):
    pre = jnp.dot(features, w_first, preferred_element_type=jnp.float32) + b_first
    sig = jax.nn.sigmoid(pre)
    dpre = (grad_out.astype(jnp.float32) * sig * (1.0 + pre * (1.0 - sig))).astype(jnp.bfloat16)
    w_grad = jnp.dot(features.T, dpre, preferred_element_type=jnp.float32)
    b_grad = jnp.sum(dpre.astype(jnp.float32), axis=0)
    lookup = lax.dot_general(dpre, w_first, (((1,), (1,)), ((), ())), preferred_element_type=jnp.float32).astype(jnp.bfloat16)
    values = lookup.reshape(-1, E).astype(jnp.float32)
    flag = admit.reshape(-1)
    rows = (owner.reshape(-1) * ADM_OWN + adm_row.reshape(-1)).astype(jnp.int32)
    rows = jnp.where(flag == 1, rows, ADM_ROWS).astype(jnp.int32)
    adm_grad = jax.ops.segment_sum(values, rows, ADM_ROWS + 1)[:ADM_ROWS]
    qrows = (q_shard.reshape(-1) * QROWS_DEV + q_local.reshape(-1)).astype(jnp.int32)
    rrows = (r_shard.reshape(-1) * QROWS_DEV + r_local.reshape(-1)).astype(jnp.int32)
    qrows = jnp.where(flag == 0, qrows, QROWS).astype(jnp.int32)
    rrows = jnp.where(flag == 0, rrows, QROWS).astype(jnp.int32)
    q_grad = jax.ops.segment_sum(values, qrows, QROWS + 1)[:QROWS]
    r_grad = jax.ops.segment_sum(values, rrows, QROWS + 1)[:QROWS]
    return (w_grad, b_grad, adm_grad, q_grad, r_grad)
```

```python
import functools

import jax
import jax.numpy as jnp
from jax import lax
from jax.experimental import pallas as pl
from jax.experimental.pallas import tpu as pltpu
from jax.sharding import PartitionSpec as P

E = 128
F = 16
SAMP = 128
HID = 1024
WROWS = 2048
QCAP = 24
CAP = 384
NDEV = 128
NOWN = 8
QROWS_DEV = 4096
OWN_ROWS = 2048
SLOTS = 3072
F32 = jnp.float32
BF16 = jnp.bfloat16
VMEM = pltpu.VMEM


def iota(shape, dim):
    return lax.broadcasted_iota(jnp.int32, shape, dim)


def onehot(cond):
    return jnp.where(cond, 1.0, 0.0).astype(BF16)


def ranks_of(dest_t, n_dest, ramp):
    hits = [onehot(iota((n_dest, SAMP), 0) == dest_t[f : f + 1, :]) for f in range(F)]
    stacked = jnp.concatenate(hits, axis=0)
    counts = jnp.dot(stacked, ramp, preferred_element_type=F32)
    base = jnp.zeros((n_dest, SAMP), F32)
    rows = []
    for f in range(F):
        part = counts[f * n_dest : (f + 1) * n_dest]
        before = part[:, :SAMP] + base
        rows.append(jnp.sum(before * hits[f].astype(F32), axis=0, keepdims=True))
        base = base + part[:, SAMP:]
    return jnp.concatenate(rows, axis=0), hits


def dense_and_buckets(feat_ref, w_ref, b_ref, g_ref, idx_ref, wl_ref, qr_ref, qlab_ref, adm_ref, alab_ref, look):
    pre = jnp.dot(feat_ref[...], w_ref[...], preferred_element_type=F32) + b_ref[...]
    sig = 1.0 / (1.0 + jnp.exp(-pre))
    dpre32 = g_ref[...].astype(F32) * sig * (1.0 + pre * (1.0 - sig))
    dpre = dpre32.astype(BF16)

    for i in range(WROWS // 256):
        block = lax.dot_general(
            feat_ref[:, i * 256 : (i + 1) * 256], dpre, (((0,), (0,)), ((), ())), preferred_element_type=F32
        )
        wl_ref[i * 256 : (i + 1) * 256, :] = block
    total = jnp.sum(dpre.astype(F32), axis=0, keepdims=True)
    wl_ref[WROWS : WROWS + 8, :] = jnp.where(iota((8, HID), 0) == 0, total, 0.0)

    for i in range(F // 2):
        part = lax.dot_general(
            dpre, w_ref[i * 256 : (i + 1) * 256, :], (((1,), (1,)), ((), ())), preferred_element_type=F32
        )
        look[2 * i] = part[:, :E]
        look[2 * i + 1] = part[:, E:]

    bucket_all(idx_ref, qr_ref, qlab_ref, adm_ref, alab_ref, look)


def bucket_all(idx_ref, qr_ref, qlab_ref, adm_ref, alab_ref, look):
    col = idx_ref[...]
    turned = jnp.transpose(col.astype(F32)).astype(jnp.int32)
    field_t = [turned[t * F : (t + 1) * F, :] for t in range(7)]
    admit_t = field_t[0]

    def field(t, f):
        return col[:, t * F + f : t * F + f + 1]

    ramp = jnp.concatenate(
        [onehot(iota((SAMP, SAMP), 0) < iota((SAMP, SAMP), 1)), jnp.ones((SAMP, SAMP), BF16)], axis=1
    )
    dest_q = jnp.where(admit_t == 0, field_t[3], -1)
    dest_r = jnp.where(admit_t == 0, field_t[5], -1)
    dest_a = jnp.where(admit_t == 1, field_t[1], -1)
    rank_q, hits_q = ranks_of(dest_q, NDEV, ramp)
    rank_r, hits_r = ranks_of(dest_r, NDEV, ramp)
    rank_a, _ = ranks_of(dest_a, 16, ramp)
    rank_col = jnp.transpose(
        jnp.concatenate([rank_q, rank_r, rank_a, jnp.zeros((SAMP - 3 * F, SAMP), F32)], axis=0)
    ).astype(jnp.int32)

    lane = iota((SAMP, 128), 1)
    parts_q, parts_r, parts_a = [], [], []
    for f in range(F):
        plain = field(0, f) == 0
        for t, at, out in ((4, 0, parts_q), (6, 64, parts_r)):
            mark = field(t, f) + 1
            rank = rank_col[:, (at // 64) * F + f : (at // 64) * F + f + 1]
            value = jnp.where(lane < at + 32, mark // 64, mark % 64)
            hit = ((lane - at == rank) | (lane - at - 32 == rank)) & plain
            out.append(jnp.where(hit, value, 0).astype(F32).astype(BF16))
        mark = field(2, f) + 1
        rank = rank_col[:, 2 * F + f : 2 * F + f + 1]
        hit = (lane == rank % 128) & (field(0, f) == 1)
        parts_a.append(
            jnp.concatenate(
                [
                    jnp.where(hit, mark // 64, 0).astype(F32).astype(BF16),
                    jnp.where(hit, mark % 64, 0).astype(F32).astype(BF16),
                ],
                axis=1,
            )
        )
    lab = jnp.dot(jnp.concatenate(hits_q, axis=1), jnp.concatenate(parts_q, axis=0), preferred_element_type=F32)
    lab = lab + jnp.dot(
        jnp.concatenate(hits_r, axis=1), jnp.concatenate(parts_r, axis=0), preferred_element_type=F32
    )
    lab = lab * 64.0 + jnp.concatenate([lab[:, 32:], lab[:, :32]], axis=1)
    qlab_ref[...] = lab.reshape(qlab_ref.shape)
    ra = rank_a.astype(jnp.int32)
    code = jnp.where(dest_a >= 0, dest_a * 3 + ra // 128, -1)
    codes = jnp.concatenate([onehot(iota((32, SAMP), 0) == code[f : f + 1, :]) for f in range(F)], axis=1)
    alab = jnp.dot(codes, jnp.concatenate(parts_a, axis=0), preferred_element_type=F32)
    alab = alab[:, :128] * 64.0 + alab[:, 128:]
    for o in range(NOWN):
        alab_ref[o] = alab[o * 3 : o * 3 + 3, :]

    def fill(slot_t, half_of, store):
        rhs = []
        for f in range(F):
            half = half_of(f)
            value = look[f]
            rhs.append(
                jnp.concatenate(
                    [jnp.where(half == 0, value, 0.0).astype(BF16), jnp.where(half == 1, value, 0.0).astype(BF16)],
                    axis=1,
                )
            )
        rhs = jnp.concatenate(rhs, axis=0)
        for m in range(8):
            want = iota((192, SAMP), 0) + m * 192
            picked = jnp.concatenate([onehot(want == slot_t[f : f + 1, :]) for f in range(F)], axis=1)
            out = jnp.dot(picked, rhs, preferred_element_type=F32)
            store(m, 0, out[:, :E])
            store(m, 1, out[:, E:])

    def store_q(at):
        def put(m, h, value):
            qr_ref[h * 64 + m * 8 : h * 64 + m * 8 + 8, at] = value.reshape(8, QCAP, E).astype(BF16)

        return put

    def store_a(m, h, value):
        owner = h * 4 + m // 2
        adm_ref[owner, (m % 2) * 192 : (m % 2) * 192 + 192, :] = value.astype(BF16)

    rq = rank_q.astype(jnp.int32)
    rr = rank_r.astype(jnp.int32)
    fill(
        jnp.where(dest_q >= 0, (dest_q % 64) * QCAP + rq, -1),
        lambda f: jnp.where(field(0, f) == 0, field(3, f) // 64, -1),
        store_q(0),
    )
    fill(
        jnp.where(dest_r >= 0, (dest_r % 64) * QCAP + rr, -1),
        lambda f: jnp.where(field(0, f) == 0, field(5, f) // 64, -1),
        store_q(1),
    )
    fill(
        jnp.where(dest_a >= 0, (dest_a % 4) * CAP + ra, -1),
        lambda f: jnp.where(field(0, f) == 1, field(1, f) // 4, -1),
        store_a,
    )


def sum_rows(marks, block, n_rows, put):
    hi_rows = n_rows // 4
    mark = marks.astype(jnp.int32) - 1
    low = jnp.where(mark >= 0, mark // hi_rows, -1)
    high = jnp.where(mark >= 0, mark % hi_rows, -1)
    low_col = jnp.transpose(
        jnp.concatenate([low.astype(F32), jnp.zeros((SAMP - 24, SAMP), F32)], axis=0)
    ).astype(jnp.int32)
    rhs = []
    for i in range(8):
        values = block(i)
        for j in range(3):
            g = i * 3 + j
            v = values[j * 128 : (j + 1) * 128]
            which = low_col[:, g : g + 1]
            rhs.append(jnp.concatenate([jnp.where(which == k, v, 0.0).astype(BF16) for k in range(4)], axis=1))
    rhs = jnp.concatenate(rhs, axis=0)
    for m in range(hi_rows // 256):
        want = iota((256, SAMP), 0) + m * 256
        picked = jnp.concatenate([onehot(want == high[g : g + 1, :]) for g in range(24)], axis=1)
        out = jnp.dot(picked, rhs, preferred_element_type=F32)
        for k in range(4):
            put(k * hi_rows + m * 256, out[:, k * E : (k + 1) * E])


def make_kernel(feat, w, b, g, idx, wl, qr, qlab, adm, alab, look):
    dense_and_buckets(feat, w, b, g, idx, wl, qr, qlab, adm, alab, look)


def qr_kernel(qr_ref, marks_ref, q_ref, r_ref):
    for t, out_ref in ((0, q_ref), (1, r_ref)):

        def put(at, value, out_ref=out_ref):
            out_ref[at : at + 256, :] = value

        sum_rows(
            marks_ref[t],
            lambda i: qr_ref[i * 16 : i * 16 + 16, t].astype(F32).reshape(384, E),
            QROWS_DEV,
            put,
        )


def adm_kernel(adm_ref, marks_ref, out_ref):
    def put(at, value):
        out_ref[at : at + 256, :] = value.astype(BF16)

    sum_rows(marks_ref[...], lambda i: adm_ref[i].astype(F32), OWN_ROWS, put)


def spec():
    return pl.BlockSpec(memory_space=VMEM)


def local(features, w_first, b_first, grad_out, admit, owner, adm_row, q_shard, q_local, r_shard, r_local):
    fields = [admit, owner[..., 0], adm_row, q_shard[..., 0], q_local, r_shard[..., 0], r_local]
    idx = jnp.concatenate(fields + [jnp.zeros((SAMP, 16), jnp.int32)], axis=1)
    wl, qr, qlab, adm, alab = pl.pallas_call(
        make_kernel,
        out_shape=(
            jax.ShapeDtypeStruct((WROWS + 8, HID), F32),
            jax.ShapeDtypeStruct((NDEV, 2, QCAP, E), BF16),
            jax.ShapeDtypeStruct((NDEV, 128), F32),
            jax.ShapeDtypeStruct((NOWN, CAP, E), BF16),
            jax.ShapeDtypeStruct((NOWN, 3, 128), F32),
        ),
        in_specs=[spec()] * 5,
        out_specs=tuple([spec()] * 5),
        scratch_shapes=[VMEM((F, SAMP, E), F32)],
        compiler_params=pltpu.CompilerParams(vmem_limit_bytes=60 << 20),
        name="dense_buckets",
    )(features, w_first, b_first.reshape(1, HID), grad_out, idx)
    adm_in = lax.all_to_all(adm, "dp", split_axis=0, concat_axis=0, tiled=True)
    alab_in = lax.all_to_all(alab, "dp", split_axis=0, concat_axis=0, tiled=True)
    qr_in = lax.all_to_all(qr, ("dp", "table"), split_axis=0, concat_axis=0, tiled=True)
    qlab_in = lax.all_to_all(qlab, ("dp", "table"), split_axis=0, concat_axis=0, tiled=True)
    owner_sums = pl.pallas_call(
        adm_kernel,
        out_shape=jax.ShapeDtypeStruct((OWN_ROWS, E), BF16),
        in_specs=[spec()] * 2,
        out_specs=spec(),
        compiler_params=pltpu.CompilerParams(vmem_limit_bytes=60 << 20),
        name="adm_sums",
    )(adm_in, alab_in.reshape(24, 128))
    adm_grad = lax.psum_scatter(owner_sums, "table", scatter_dimension=0, tiled=True).astype(F32)
    marks = jnp.stack([qlab_in[:, :QCAP].reshape(24, 128), qlab_in[:, 64 : 64 + QCAP].reshape(24, 128)])
    q_grad, r_grad = pl.pallas_call(
        qr_kernel,
        out_shape=(jax.ShapeDtypeStruct((QROWS_DEV, E), F32), jax.ShapeDtypeStruct((QROWS_DEV, E), F32)),
        in_specs=[spec()] * 2,
        out_specs=(spec(), spec()),
        compiler_params=pltpu.CompilerParams(vmem_limit_bytes=60 << 20),
        name="qr_sums",
    )(qr_in, marks)
    summed = lax.psum(wl, ("dp", "table"))
    w_grad = summed[:WROWS]
    b_grad = summed[WROWS]
    return (w_grad, b_grad, adm_grad, q_grad, r_grad)


def solution(mesh):
    both = ("dp", "table")
    two, three = P(both, None), P(both, None, None)
    return jax.shard_map(
        local,
        mesh=mesh,
        in_specs=(two, P(), P(), two, two, three, two, three, two, three, two),
        out_specs=(P(), P(), two, two, two),
        check_vma=False,
    )
```

```python
import functools

import jax
import jax.numpy as jnp
from jax import lax
from jax.experimental import pallas as pl
from jax.experimental.pallas import tpu as pltpu
from jax.sharding import PartitionSpec as P

E = 128
F = 16
SAMP = 128
HID = 1024
WROWS = 2048
QCAP = 24
CAP = 384
NDEV = 128
NOWN = 8
QROWS_DEV = 4096
OWN_ROWS = 2048
SLOTS = 3072
HALF = 1024
HALF_ROWS = 8192
F32 = jnp.float32
BF16 = jnp.bfloat16
VMEM = pltpu.VMEM


def iota(shape, dim):
    return lax.broadcasted_iota(jnp.int32, shape, dim)


def onehot(cond):
    return jnp.where(cond, 1.0, 0.0).astype(BF16)


def ranks_of(dest_t, n_dest, ramp):
    hits = [onehot(iota((n_dest, SAMP), 0) == dest_t[f : f + 1, :]) for f in range(F)]
    stacked = jnp.concatenate(hits, axis=0)
    counts = jnp.dot(stacked, ramp, preferred_element_type=F32)
    base = jnp.zeros((n_dest, SAMP), F32)
    rows = []
    for f in range(F):
        part = counts[f * n_dest : (f + 1) * n_dest]
        before = part[:, :SAMP] + base
        rows.append(jnp.sum(before * hits[f].astype(F32), axis=0, keepdims=True))
        base = base + part[:, SAMP:]
    return jnp.concatenate(rows, axis=0), hits


def dense_and_buckets(feat_ref, w_ref, b_ref, g_ref, fields, own_ref, other_ref, bl_ref, qr_ref, qlab_ref, adm_ref, alab_ref, look):
    core = lax.rem(lax.axis_index("dp"), 2)
    pre = jnp.dot(feat_ref[...], w_ref[...], preferred_element_type=F32) + b_ref[...]
    sig = 1.0 / (1.0 + jnp.exp(-pre))
    dpre32 = g_ref[...].astype(F32) * sig * (1.0 + pre * (1.0 - sig))
    dpre = dpre32.astype(BF16)

    for half, out_ref in ((1 - core, other_ref), (core, own_ref)):
        for i in range(HALF // 256):
            at = pl.multiple_of(half * HALF + i * 256, 256)
            block = lax.dot_general(
                feat_ref[:, pl.ds(at, 256)], dpre, (((0,), (0,)), ((), ())), preferred_element_type=F32
            )
            for k in range(HID // 128):
                out_ref[k * HALF + i * 256 : k * HALF + i * 256 + 256, :] = block[:, k * 128 : k * 128 + 128].astype(
                    out_ref.dtype
                )
    total = jnp.sum(dpre.astype(F32), axis=0, keepdims=True)
    for k in range(HID // 128):
        bl_ref[k : k + 1, :] = total[:, k * 128 : k * 128 + 128]

    for i in range(F // 2):
        part = lax.dot_general(
            dpre, w_ref[i * 256 : (i + 1) * 256, :], (((1,), (1,)), ((), ())), preferred_element_type=F32
        )
        look[2 * i] = part[:, :E]
        look[2 * i + 1] = part[:, E:]

    bucket_all(fields, qr_ref, qlab_ref, adm_ref, alab_ref, look)


def bucket_all(fields, qr_ref, qlab_ref, adm_ref, alab_ref, look):
    field_t = [ref[...] if len(ref.shape) == 2 else ref[:, 0, :] for ref in fields]
    admit_t = field_t[0]
    stacked = jnp.concatenate([t.astype(F32) for t in field_t] + [jnp.zeros((F, SAMP), F32)], axis=0)
    col = jnp.transpose(stacked).astype(jnp.int32)

    def field(t, f):
        return col[:, t * F + f : t * F + f + 1]

    ramp = jnp.concatenate(
        [onehot(iota((SAMP, SAMP), 0) < iota((SAMP, SAMP), 1)), jnp.ones((SAMP, SAMP), BF16)], axis=1
    )
    dest_q = jnp.where(admit_t == 0, field_t[3], -1)
    dest_r = jnp.where(admit_t == 0, field_t[5], -1)
    dest_a = jnp.where(admit_t == 1, field_t[1], -1)
    rank_q, hits_q = ranks_of(dest_q, NDEV, ramp)
    rank_r, hits_r = ranks_of(dest_r, NDEV, ramp)
    rank_a, _ = ranks_of(dest_a, 16, ramp)
    rank_col = jnp.transpose(
        jnp.concatenate([rank_q, rank_r, rank_a, jnp.zeros((SAMP - 3 * F, SAMP), F32)], axis=0)
    ).astype(jnp.int32)

    lane = iota((SAMP, 128), 1)
    parts_q, parts_r, parts_a = [], [], []
    for f in range(F):
        plain = field(0, f) == 0
        for t, at, out in ((4, 0, parts_q), (6, 64, parts_r)):
            mark = field(t, f) + 1
            rank = rank_col[:, (at // 64) * F + f : (at // 64) * F + f + 1]
            value = jnp.where(lane < at + 32, mark // 64, mark % 64)
            hit = ((lane - at == rank) | (lane - at - 32 == rank)) & plain
            out.append(jnp.where(hit, value, 0).astype(F32).astype(BF16))
        mark = field(2, f) + 1
        rank = rank_col[:, 2 * F + f : 2 * F + f + 1]
        hit = (lane == rank % 128) & (field(0, f) == 1)
        parts_a.append(
            jnp.concatenate(
                [
                    jnp.where(hit, mark // 64, 0).astype(F32).astype(BF16),
                    jnp.where(hit, mark % 64, 0).astype(F32).astype(BF16),
                ],
                axis=1,
            )
        )
    lab = jnp.dot(jnp.concatenate(hits_q, axis=1), jnp.concatenate(parts_q, axis=0), preferred_element_type=F32)
    lab = lab + jnp.dot(
        jnp.concatenate(hits_r, axis=1), jnp.concatenate(parts_r, axis=0), preferred_element_type=F32
    )
    lab = lab * 64.0 + jnp.concatenate([lab[:, 32:], lab[:, :32]], axis=1)
    qlab_ref[...] = lab.reshape(qlab_ref.shape)
    ra = rank_a.astype(jnp.int32)
    code = jnp.where(dest_a >= 0, dest_a * 3 + ra // 128, -1)
    codes = jnp.concatenate([onehot(iota((32, SAMP), 0) == code[f : f + 1, :]) for f in range(F)], axis=1)
    alab = jnp.dot(codes, jnp.concatenate(parts_a, axis=0), preferred_element_type=F32)
    alab = alab[:, :128] * 64.0 + alab[:, 128:]
    for o in range(NOWN):
        alab_ref[o] = alab[o * 3 : o * 3 + 3, :]

    def fill(slot_t, half_of, store):
        rhs = []
        for f in range(F):
            half = half_of(f)
            value = look[f]
            rhs.append(
                jnp.concatenate(
                    [jnp.where(half == 0, value, 0.0).astype(BF16), jnp.where(half == 1, value, 0.0).astype(BF16)],
                    axis=1,
                )
            )
        rhs = jnp.concatenate(rhs, axis=0)
        for m in range(8):
            want = iota((192, SAMP), 0) + m * 192
            picked = jnp.concatenate([onehot(want == slot_t[f : f + 1, :]) for f in range(F)], axis=1)
            out = jnp.dot(picked, rhs, preferred_element_type=F32)
            store(m, 0, out[:, :E])
            store(m, 1, out[:, E:])

    def store_q(at):
        def put(m, h, value):
            qr_ref[h * 64 + m * 8 : h * 64 + m * 8 + 8, at] = value.reshape(8, QCAP, E).astype(BF16)

        return put

    def store_a(m, h, value):
        owner = h * 4 + m // 2
        adm_ref[owner, (m % 2) * 192 : (m % 2) * 192 + 192, :] = value.astype(BF16)

    rq = rank_q.astype(jnp.int32)
    rr = rank_r.astype(jnp.int32)
    fill(
        jnp.where(dest_q >= 0, (dest_q % 64) * QCAP + rq, -1),
        lambda f: jnp.where(field(0, f) == 0, field(3, f) // 64, -1),
        store_q(0),
    )
    fill(
        jnp.where(dest_r >= 0, (dest_r % 64) * QCAP + rr, -1),
        lambda f: jnp.where(field(0, f) == 0, field(5, f) // 64, -1),
        store_q(1),
    )
    fill(
        jnp.where(dest_a >= 0, (dest_a % 4) * CAP + ra, -1),
        lambda f: jnp.where(field(0, f) == 1, field(1, f) // 4, -1),
        store_a,
    )


def sum_rows(marks, block, n_rows, put):
    hi_rows = n_rows // 4
    mark = marks.astype(jnp.int32) - 1
    low = jnp.where(mark >= 0, mark // hi_rows, -1)
    high = jnp.where(mark >= 0, mark % hi_rows, -1)
    low_col = jnp.transpose(
        jnp.concatenate([low.astype(F32), jnp.zeros((SAMP - 24, SAMP), F32)], axis=0)
    ).astype(jnp.int32)
    rhs = []
    for i in range(8):
        values = block(i)
        for j in range(3):
            g = i * 3 + j
            v = values[j * 128 : (j + 1) * 128]
            which = low_col[:, g : g + 1]
            rhs.append(jnp.concatenate([jnp.where(which == k, v, 0.0).astype(BF16) for k in range(4)], axis=1))
    rhs = jnp.concatenate(rhs, axis=0)
    for m in range(hi_rows // 256):
        want = iota((256, SAMP), 0) + m * 256
        picked = jnp.concatenate([onehot(want == high[g : g + 1, :]) for g in range(24)], axis=1)
        out = jnp.dot(picked, rhs, preferred_element_type=F32)
        for k in range(4):
            put(k * hi_rows + m * 256, out[:, k * E : (k + 1) * E])


MESH = pl.DeviceIdType.MESH
STREAMS = ((3072, 0, (0, 1, 2)), (3072, 3072, (1, 2, 0)), (2048, 6144, (2, 0, 1)))


def piece(stream, stage):
    return STREAMS[stream][0] // 4 ** (stage + 1)


def stage_rows():
    table, at = {}, 0
    for stage in range(3):
        for stream in range(3):
            table[stage, stream] = at
            at += 3 * piece(stream, stage)
    return table, at


ROWS_AT, ROWS_ALL = stage_rows()
GAPS = (0, 6, 17, 17, 17, 17, 17, 17, 17, 2, 0, 0)


def comm_kernel(
    own_ref, other_ref, bl_ref, qr_ref, qlab_ref, adm_ref, alab_ref,
    full_ref, bout_ref, qr_in, qlab_in, agrad_ref,
    pair_in, data, sbuf, rbuf, bsum, adm_in, alab_in, osum, osum_in,
    pair_sem, rs_sem, ag_sem, fw_sem, b_sem, adm_sem, qr_sem, tab_sem,
):
    dp, tab = lax.axis_index("dp"), lax.axis_index("table")
    core, x = lax.rem(dp, 2), lax.div(dp, 2)
    y, z = lax.div(tab, 4), lax.rem(tab, 4)
    me = dp * 16 + tab
    place = (x, y, z)

    def turn(value, step):
        return lax.rem(value + step + 4, 4)

    def beside(axis, step):
        if axis == 0:
            return (turn(x, step) * 2 + core, tab)
        if axis == 1:
            return (dp, turn(y, step) * 4 + z)
        return (dp, y * 4 + turn(z, step))

    partner = (dp + 1 - 2 * core, tab)

    def remote(src, dst, sems, device):
        return pltpu.make_async_remote_copy(
            src_ref=src, dst_ref=dst, send_sem=sems[0], recv_sem=sems[1], device_id=device, device_id_type=MESH
        )

    def sems(array, *at):
        return array.at[(0,) + at], array.at[(1,) + at]

    barrier = pltpu.get_barrier_semaphore()

    @pl.loop(1, NDEV)
    def _(i):
        peer = lax.rem(me + i, NDEV)
        pl.semaphore_signal(
            barrier, inc=1, device_id=(lax.div(peer, 16), lax.rem(peer, 16)), device_id_type=MESH
        )

    pl.semaphore_wait(barrier, NDEV - 1)

    def start_adm():
        for i in range(1, NOWN):
            peer = lax.rem(dp + i, NOWN)
            remote(adm_ref.at[peer], adm_in.at[dp], sems(adm_sem, 0), (peer, tab)).start()
            remote(alab_ref.at[peer], alab_in.at[dp], sems(adm_sem, 1), (peer, tab)).start()
        adm_in[dp] = adm_ref[dp]
        alab_in[dp] = alab_ref[dp]

    def wait_all(src, dst, array, at):
        pltpu.make_async_copy(src, src, array.at[(0,) + at]).wait()
        pltpu.make_async_copy(dst, dst, array.at[(1,) + at]).wait()

    def sum_adm():
        wait_all(adm_ref.at[0:7], adm_in.at[0:7], adm_sem, (0,))
        wait_all(alab_ref.at[0:7], alab_in.at[0:7], adm_sem, (1,))

        def put(at, value):
            for j in range(2):
                osum[at // 128 + j] = value[j * 128 : j * 128 + 128].astype(BF16)

        marks = jnp.concatenate([alab_in[o] for o in range(NOWN)], axis=0)
        sum_rows(marks, lambda i: adm_in[i].astype(F32), OWN_ROWS, put)

        @pl.loop(1, 16)
        def _(i):
            peer = lax.rem(tab + i, 16)
            remote(osum.at[peer], osum_in.at[tab], sems(tab_sem), (dp, peer)).start()

        osum_in[tab] = osum[tab]

    def finish_adm():
        wait_all(osum.at[0:15], osum_in.at[0:15], tab_sem, ())
        total = osum_in[0].astype(F32)
        for j in range(1, 16):
            total = total + osum_in[j].astype(F32)
        agrad_ref[...] = total

    def start_qr(first, count):
        @pl.loop(first, first + count)
        def _(i):
            peer = lax.rem(me + i, NDEV)
            device = (lax.div(peer, 16), lax.rem(peer, 16))
            remote(qr_ref.at[peer], qr_in.at[me], sems(qr_sem, 0), device).start()
            remote(qlab_ref.at[peer], qlab_in.at[me], sems(qr_sem, 1), device).start()

    sent = [1]

    def gap(k):
        if GAPS[k]:
            start_qr(sent[0], GAPS[k])
            sent[0] += GAPS[k]

    bias_slots = ((0, 2, core), (2, 4, x), (6, 4, y), (10, 4, z))

    def bias_start(k):
        first, count, mine = bias_slots[k]
        slot = first + mine
        for i in range(1, count):
            device = partner if k == 0 else beside(k - 1, i)
            remote(bsum.at[slot], bsum.at[slot], sems(b_sem, first + i), device).start()

    def bias_wait(k):
        first, count, mine = bias_slots[k]
        for i in range(1, count):
            pltpu.make_async_copy(bsum.at[first], bsum.at[first], b_sem.at[0, first + i]).wait()
            pltpu.make_async_copy(bsum.at[first], bsum.at[first], b_sem.at[1, first + i]).wait()
        total = bsum[first]
        for i in range(1, count):
            total = total + bsum[first + i]
        return total

    pair = remote(other_ref, pair_in, sems(pair_sem), partner)
    pair.start()
    bsum[bias_slots[0][0] + core] = bl_ref[...]
    bias_start(0)
    start_adm()
    qr_in[me] = qr_ref[me]
    qlab_in[me] = qlab_ref[me]
    pair.wait()

    @pl.loop(0, 16)
    def _(i):
        rows = pl.ds(pl.multiple_of(i * 512, 512), 512)
        data[rows, :] = own_ref[rows, :] + pair_in[rows, :].astype(F32)

    first_row = [pl.multiple_of(jnp.int32(0) + STREAMS[k][1], 16) for k in range(3)]
    starts = [[], [], []]
    gap_at = 0
    fillers = {1: sum_adm, 6: finish_adm}
    for stage in range(3):
        copies = []
        for k in range(3):
            n, p = piece(k, stage), place[STREAMS[k][2][stage]]
            axis, h, at, cur = STREAMS[k][2][stage], piece(k, stage) // 2, ROWS_AT[stage, k], first_row[k]
            far = data[pl.ds(pl.multiple_of(cur + turn(p, 2) * n, 16), n), :].astype(BF16)
            sbuf[at : at + n, :] = far
            for d, step in ((0, 1), (1, -1)):
                part = slice(at + d * h, at + d * h + h)
                copies.append(remote(sbuf.at[part], rbuf.at[part], sems(rs_sem, stage, k, d), beside(axis, step)))
                copies[-1].start()
        if stage == 0:
            total = bias_wait(0)
            bsum[2 + x] = total
            bias_start(1)
        gap(gap_at)
        gap_at += 1
        for copy in copies:
            copy.wait()
        copies = []
        for k in range(3):
            n, p = piece(k, stage), place[STREAMS[k][2][stage]]
            axis, h, at, cur = STREAMS[k][2][stage], piece(k, stage) // 2, ROWS_AT[stage, k], first_row[k]
            for d, step in ((0, 1), (1, -1)):
                row = pl.multiple_of(cur + turn(p, step) * n, 16)
                to = at + n + d * n
                for e in range(2):
                    value = data[pl.ds(row + e * h, h), :]
                    if e == d:
                        value = value + rbuf[at + d * h : at + d * h + h, :].astype(F32)
                    sbuf[to + e * h : to + e * h + h, :] = value.astype(BF16)
                part = slice(to, to + n)
                copies.append(remote(sbuf.at[part], rbuf.at[part], sems(rs_sem, stage, k, 2 + d), beside(axis, step)))
                copies[-1].start()
        gap(gap_at)
        if gap_at in fillers:
            fillers[gap_at]()
        gap_at += 1
        for copy in copies:
            copy.wait()
        if stage < 2:
            total = bias_wait(stage + 1)
            bsum[bias_slots[stage + 2][0] + bias_slots[stage + 2][2]] = total
            bias_start(stage + 2)
        else:
            bout_ref[...] = bias_wait(3)
        for k in range(3):
            n, p = piece(k, stage), place[STREAMS[k][2][stage]]
            at, cur = ROWS_AT[stage, k], first_row[k]
            mine = pl.multiple_of(cur + p * n, 16)
            value = data[pl.ds(mine, n), :]
            value = value + rbuf[at + n : at + 2 * n, :].astype(F32) + rbuf[at + 2 * n : at + 3 * n, :].astype(F32)
            if stage < 2:
                data[pl.ds(mine, n), :] = value
            else:
                full_ref[core, pl.ds(mine, n), :] = value.astype(BF16)
            starts[k].append(cur)
            first_row[k] = mine

    forwards = []

    def forward(k, which, row, n):
        rows = pl.ds(pl.multiple_of(row, 16), n)
        forwards.append(
            remote(full_ref.at[core, rows], full_ref.at[core, rows], sems(fw_sem, k, which), partner)
        )
        forwards[-1].start()

    for stage in (2, 1, 0):
        copies = []
        for k in range(3):
            n, axis = piece(k, stage), STREAMS[k][2][stage]
            p, cur = place[axis], starts[k][stage]
            rows = pl.ds(pl.multiple_of(cur + p * n, 16), n)
            for d, step in ((0, 1), (1, -1)):
                copies.append(
                    remote(full_ref.at[core, rows], full_ref.at[core, rows], sems(ag_sem, stage, k, d), beside(axis, step))
                )
                copies[-1].start()
            if stage == 0:
                forward(k, 0, cur + p * n, n)
        gap(gap_at)
        if gap_at in fillers:
            fillers[gap_at]()
        gap_at += 1
        for copy in copies:
            copy.wait()
        copies = []
        for k in range(3):
            n, axis = piece(k, stage), STREAMS[k][2][stage]
            p, cur, h = place[axis], starts[k][stage], piece(k, stage) // 2
            for d, step in ((0, 1), (1, -1)):
                rows = pl.ds(pl.multiple_of(cur + turn(p, -step) * n + d * h, 8), h)
                copies.append(
                    remote(
                        full_ref.at[core, rows], full_ref.at[core, rows], sems(ag_sem, stage, k, 2 + d), beside(axis, step)
                    )
                )
                copies[-1].start()
            if stage == 0:
                forward(k, 1, cur + turn(p, 1) * n, n)
                forward(k, 2, cur + turn(p, -1) * n, n)
        gap(gap_at)
        gap_at += 1
        for copy in copies:
            copy.wait()
        if stage == 0:
            for k in range(3):
                n = piece(k, 0)
                forward(k, 3, starts[k][0] + turn(place[STREAMS[k][2][0]], 2) * n, n)
    for copy in forwards:
        copy.wait()
    wait_all(qr_ref.at[0 : NDEV - 1], qr_in.at[0 : NDEV - 1], qr_sem, (0,))
    wait_all(qlab_ref.at[0 : NDEV - 1], qlab_in.at[0 : NDEV - 1], qr_sem, (1,))


def make_kernel(feat, w, b, g, *refs):
    dense_and_buckets(feat, w, b, g, refs[:7], *refs[7:])


def finish_kernel(qr_ref, marks_ref, full_ref, q_ref, r_ref, w_ref, stage, sem):
    copies = []

    def widen(i):
        half, row = i // 4, i % 4 * 256
        for k in range(HID // 128):
            at = k * HALF + row
            stage[i * 256 : i * 256 + 256, k * 128 : k * 128 + 128] = full_ref[half, at : at + 256, :].astype(F32)
        rows = slice(i * 256, i * 256 + 256)
        copies.append(pltpu.make_async_copy(stage.at[rows], w_ref.at[rows], sem.at[i]))
        copies[-1].start()

    for i in range(8):
        widen(i)
    for t, out_ref in ((0, q_ref), (1, r_ref)):

        def put(at, value, out_ref=out_ref):
            out_ref[at : at + 256, :] = value

        sum_rows(
            marks_ref[t],
            lambda i: qr_ref[i * 16 : i * 16 + 16, t].astype(F32).reshape(384, E),
            QROWS_DEV,
            put,
        )
    for copy in copies:
        copy.wait()


def spec():
    return pl.BlockSpec(memory_space=VMEM)


def shape(dims, dtype):
    return jax.ShapeDtypeStruct(dims, dtype)


def local(features, w_first, b_first, grad_out, admit, owner, adm_row, q_shard, q_local, r_shard, r_local):
    fields = [
        f.T if f.ndim == 2 else f.transpose(1, 2, 0)
        for f in (admit, owner, adm_row, q_shard, q_local, r_shard, r_local)
    ]
    room = 60 << 20
    made = pl.pallas_call(
        make_kernel,
        out_shape=(
            shape((HALF_ROWS, 128), F32),
            shape((HALF_ROWS, 128), BF16),
            shape((8, 128), F32),
            shape((NDEV, 2, QCAP, E), BF16),
            shape((NDEV, 1, 128), F32),
            shape((NOWN, CAP, E), BF16),
            shape((NOWN, 3, 128), F32),
        ),
        in_specs=[spec()] * 11,
        out_specs=tuple([spec()] * 7),
        scratch_shapes=[VMEM((F, SAMP, E), F32)],
        compiler_params=pltpu.CompilerParams(vmem_limit_bytes=room),
        name="dense_buckets",
    )(features, w_first, b_first.reshape(1, HID), grad_out, *fields)
    dma = pltpu.SemaphoreType.DMA
    full, b_sum, qr_in, qlab_in, adm_grad = pl.pallas_call(
        comm_kernel,
        out_shape=(
            shape((2, HALF_ROWS, 128), BF16),
            shape((8, 128), F32),
            shape((NDEV, 2, QCAP, E), BF16),
            shape((NDEV, 1, 128), F32),
            shape((128, E), F32),
        ),
        in_specs=[spec()] * 7,
        out_specs=tuple([spec()] * 5),
        scratch_shapes=[
            VMEM((HALF_ROWS, 128), BF16),
            VMEM((HALF_ROWS, 128), F32),
            VMEM((ROWS_ALL, 128), BF16),
            VMEM((ROWS_ALL, 128), BF16),
            VMEM((14, 8, 128), F32),
            VMEM((NOWN, CAP, E), BF16),
            VMEM((NOWN, 3, 128), F32),
            VMEM((16, 128, E), BF16),
            VMEM((16, 128, E), BF16),
            dma((2,)),
            dma((2, 3, 3, 4)),
            dma((2, 3, 3, 4)),
            dma((2, 3, 4)),
            dma((2, 14)),
            dma((2, 2)),
            dma((2, 2)),
            dma((2,)),
        ],
        compiler_params=pltpu.CompilerParams(vmem_limit_bytes=room, collective_id=0, has_side_effects=True),
        name="exchange",
    )(*made)
    marks = jnp.stack([qlab_in[:, 0, :QCAP].reshape(24, 128), qlab_in[:, 0, 64 : 64 + QCAP].reshape(24, 128)])
    q_grad, r_grad, w_grad = pl.pallas_call(
        finish_kernel,
        out_shape=(shape((QROWS_DEV, E), F32), shape((QROWS_DEV, E), F32), shape((WROWS, HID), F32)),
        in_specs=[spec()] * 3,
        out_specs=(spec(), spec(), pl.BlockSpec(memory_space=pl.ANY)),
        scratch_shapes=[VMEM((WROWS, HID), F32), dma((8,))],
        compiler_params=pltpu.CompilerParams(vmem_limit_bytes=room),
        name="finish",
    )(qr_in, marks, full)
    return (w_grad, b_sum.reshape(HID), adm_grad, q_grad, r_grad)


def solution(mesh):
    both = ("dp", "table")
    two, three = P(both, None), P(both, None, None)
    return jax.shard_map(
        local,
        mesh=mesh,
        in_specs=(two, P(), P(), two, two, three, two, three, two, three, two),
        out_specs=(P(), P(), two, two, two),
        check_vma=False,
    )
```

```python
import functools

import jax
import jax.numpy as jnp
from jax import lax
from jax.experimental import pallas as pl
from jax.experimental.pallas import tpu as pltpu
from jax.sharding import PartitionSpec as P

E = 128
F = 16
SAMP = 128
HID = 1024
WROWS = 2048
QCAP = 24
CAP = 384
NDEV = 128
NOWN = 8
QROWS_DEV = 4096
OWN_ROWS = 2048
SLOTS = 3072
HALF = 1024
HALF_ROWS = 8192
F32 = jnp.float32
BF16 = jnp.bfloat16
VMEM = pltpu.VMEM


def iota(shape, dim):
    return lax.broadcasted_iota(jnp.int32, shape, dim)


def onehot(cond):
    return jnp.where(cond, 1.0, 0.0).astype(BF16)


def ranks_of(dest_t, n_dest, ramp):
    hits = [onehot(iota((n_dest, SAMP), 0) == dest_t[f : f + 1, :]) for f in range(F)]
    stacked = jnp.concatenate(hits, axis=0)
    counts = jnp.dot(stacked, ramp, preferred_element_type=F32)
    base = jnp.zeros((n_dest, SAMP), F32)
    rows = []
    for f in range(F):
        part = counts[f * n_dest : (f + 1) * n_dest]
        before = part[:, :SAMP] + base
        rows.append(jnp.sum(before * hits[f].astype(F32), axis=0, keepdims=True))
        base = base + part[:, SAMP:]
    return jnp.concatenate(rows, axis=0), hits


def fields_of(fields):
    field_t = [ref[...] if len(ref.shape) == 2 else ref[:, 0, :] for ref in fields]
    stacked = jnp.concatenate([t.astype(F32) for t in field_t] + [jnp.zeros((F, SAMP), F32)], axis=0)
    return field_t, jnp.transpose(stacked).astype(jnp.int32)


def ramp_of():
    return jnp.concatenate(
        [onehot(iota((SAMP, SAMP), 0) < iota((SAMP, SAMP), 1)), jnp.ones((SAMP, SAMP), BF16)], axis=1
    )


def as_columns(rank_t):
    return jnp.transpose(jnp.concatenate([rank_t, jnp.zeros((SAMP - F, SAMP), F32)], axis=0)).astype(jnp.int32)


def fill(look, slot_t, half_of, store):
    rhs = []
    for f in range(F):
        half = half_of(f)
        value = look[f]
        rhs.append(
            jnp.concatenate(
                [jnp.where(half == 0, value, 0.0).astype(BF16), jnp.where(half == 1, value, 0.0).astype(BF16)],
                axis=1,
            )
        )
    rhs = jnp.concatenate(rhs, axis=0)
    for m in range(8):
        want = iota((192, SAMP), 0) + m * 192
        picked = jnp.concatenate([onehot(want == slot_t[f : f + 1, :]) for f in range(F)], axis=1)
        out = jnp.dot(picked, rhs, preferred_element_type=F32)
        store(m, 0, out[:, :E])
        store(m, 1, out[:, E:])


def bucket_adm(fields, adm_ref, alab_ref, look):
    field_t, col = fields_of(fields)

    def field(t, f):
        return col[:, t * F + f : t * F + f + 1]

    dest = jnp.where(field_t[0] == 1, field_t[1], -1)
    rank_t, _ = ranks_of(dest, 16, ramp_of())
    rank_col = as_columns(rank_t)
    lane = iota((SAMP, 128), 1)
    parts = []
    for f in range(F):
        mark = field(2, f) + 1
        hit = (lane == rank_col[:, f : f + 1] % 128) & (field(0, f) == 1)
        parts.append(
            jnp.concatenate(
                [
                    jnp.where(hit, mark // 64, 0).astype(F32).astype(BF16),
                    jnp.where(hit, mark % 64, 0).astype(F32).astype(BF16),
                ],
                axis=1,
            )
        )
    rank = rank_t.astype(jnp.int32)
    code = jnp.where(dest >= 0, dest * 3 + rank // 128, -1)
    codes = jnp.concatenate([onehot(iota((32, SAMP), 0) == code[f : f + 1, :]) for f in range(F)], axis=1)
    alab = jnp.dot(codes, jnp.concatenate(parts, axis=0), preferred_element_type=F32)
    alab = alab[:, :128] * 64.0 + alab[:, 128:]
    for o in range(NOWN):
        alab_ref[o] = alab[o * 3 : o * 3 + 3, :]

    def store(m, h, value):
        adm_ref[h * 4 + m // 2, (m % 2) * 192 : (m % 2) * 192 + 192, :] = value.astype(BF16)

    fill(
        look,
        jnp.where(dest >= 0, (dest % 4) * CAP + rank, -1),
        lambda f: jnp.where(field(0, f) == 1, field(1, f) // 4, -1),
        store,
    )


def bucket_plain(fields, table, qr_ref, lab_ref, look):
    field_t, col = fields_of(fields)

    def field(t, f):
        return col[:, t * F + f : t * F + f + 1]

    shard, row, at = 3 + 2 * table, 4 + 2 * table, 64 * table
    dest = jnp.where(field_t[0] == 0, field_t[shard], -1)
    rank_t, hits = ranks_of(dest, NDEV, ramp_of())
    rank_col = as_columns(rank_t)
    lane = iota((SAMP, 128), 1)
    parts = []
    for f in range(F):
        mark = field(row, f) + 1
        rank = rank_col[:, f : f + 1]
        value = jnp.where(lane < at + 32, mark // 64, mark % 64)
        hit = ((lane - at == rank) | (lane - at - 32 == rank)) & (field(0, f) == 0)
        parts.append(jnp.where(hit, value, 0).astype(F32).astype(BF16))
    lab = jnp.dot(jnp.concatenate(hits, axis=1), jnp.concatenate(parts, axis=0), preferred_element_type=F32)
    lab = lab.reshape(lab_ref.shape)
    lab_ref[...] = lab if table == 0 else lab_ref[...] + lab

    def store(m, h, value):
        qr_ref[h * 64 + m * 8 : h * 64 + m * 8 + 8, table] = value.reshape(8, QCAP, E).astype(BF16)

    fill(
        look,
        jnp.where(dest >= 0, (dest % 64) * QCAP + rank_t.astype(jnp.int32), -1),
        lambda f: jnp.where(field(0, f) == 0, field(shard, f) // 64, -1),
        store,
    )


def flat_marks(lab):
    slot = iota((128, 1536), 1)
    inner = slot % 384
    spread = onehot(iota((128, 1536), 0) == (slot // 384) * 32 + inner % QCAP)
    wide = jnp.dot(lab.astype(BF16), spread, preferred_element_type=F32)
    wide = jnp.where(inner // QCAP == iota((128, 1536), 0) % 16, wide, 0.0).astype(BF16)
    gather = onehot(iota((16, 128), 0) == iota((16, 128), 1) // 16)
    flat = jnp.dot(gather, wide, preferred_element_type=F32)[:8]
    return [flat[:, t * 768 : t * 768 + 384] * 64.0 + flat[:, t * 768 + 384 : t * 768 + 768] for t in range(2)]


def sum_rows(marks, group, block, n_rows, put):
    hi_rows = n_rows // 4
    mark = marks.astype(jnp.int32) - 1
    low = jnp.where(mark >= 0, mark // hi_rows, -1)
    high = jnp.where(mark >= 0, mark % hi_rows, -1)
    low_col = jnp.transpose(
        jnp.concatenate([low.astype(F32), jnp.zeros((SAMP - 24, SAMP), F32)], axis=0)
    ).astype(jnp.int32)
    order = [group(i, j) for i in range(8) for j in range(3)]
    rhs = []
    for i in range(8):
        values = block(i)
        for j in range(3):
            g = group(i, j)
            v = values[j * 128 : (j + 1) * 128]
            which = low_col[:, g : g + 1]
            rhs.append(jnp.concatenate([jnp.where(which == k, v, 0.0).astype(BF16) for k in range(4)], axis=1))
    rhs = jnp.concatenate(rhs, axis=0)
    for m in range(hi_rows // 256):
        want = iota((256, SAMP), 0) + m * 256
        picked = jnp.concatenate([onehot(want == high[g : g + 1, :]) for g in order], axis=1)
        out = jnp.dot(picked, rhs, preferred_element_type=F32)
        for k in range(4):
            put(k * hi_rows + m * 256, out[:, k * E : (k + 1) * E])


MESH = pl.DeviceIdType.MESH
STREAMS = ((3072, 0, (0, 1, 2)), (3072, 3072, (1, 2, 0)), (2048, 6144, (2, 0, 1)))


def piece(stream, stage):
    return STREAMS[stream][0] // 4 ** (stage + 1)


def stage_rows():
    table, at = {}, 0
    for stage in range(3):
        for stream in range(3):
            table[stage, stream] = at
            at += 3 * piece(stream, stage)
    return table, at


ROWS_AT, ROWS_ALL = stage_rows()
GAPS = (0, 0, 18, 18, 18, 18, 18, 18, 19, 0, 0, 0)


def step_kernel(
    feat_ref, w_ref, b_ref, g_ref, f0, f1, f2, f3, f4, f5, f6,
    full_ref, bout_ref, agrad_ref, q_ref, r_ref,
    feat_in, dpre_ref, dpre_in, data, look, sbuf, rbuf, bsum,
    qr_ref, qr_in, qlab_ref, qlab_in, adm_ref, adm_in, alab_ref, alab_in, osum, osum_in,
    pair_sem, rs_sem, ag_sem, fw_sem, b_sem, adm_sem, qr_sem, tab_sem,
):
    dp, tab = lax.axis_index("dp"), lax.axis_index("table")
    core, x = lax.rem(dp, 2), lax.div(dp, 2)
    y, z = lax.div(tab, 4), lax.rem(tab, 4)
    me = dp * 16 + tab
    place = (x, y, z)

    def turn(value, step):
        return lax.rem(value + step + 4, 4)

    def beside(axis, step):
        if axis == 0:
            return (turn(x, step) * 2 + core, tab)
        if axis == 1:
            return (dp, turn(y, step) * 4 + z)
        return (dp, y * 4 + turn(z, step))

    partner = (dp + 1 - 2 * core, tab)

    def remote(src, dst, sems, device):
        return pltpu.make_async_remote_copy(
            src_ref=src, dst_ref=dst, send_sem=sems[0], recv_sem=sems[1], device_id=device, device_id_type=MESH
        )

    def sems(array, *at):
        return array.at[(0,) + at], array.at[(1,) + at]

    barrier = pltpu.get_barrier_semaphore()

    @pl.loop(1, NDEV)
    def _(i):
        peer = lax.rem(me + i, NDEV)
        pl.semaphore_signal(
            barrier, inc=1, device_id=(lax.div(peer, 16), lax.rem(peer, 16)), device_id_type=MESH
        )

    fields = (f0, f1, f2, f3, f4, f5, f6)
    pre = jnp.dot(feat_ref[...], w_ref[...], preferred_element_type=F32) + b_ref[...]
    sig = 1.0 / (1.0 + jnp.exp(-pre))
    dpre_ref[...] = (g_ref[...].astype(F32) * sig * (1.0 + pre * (1.0 - sig))).astype(BF16)
    pl.semaphore_wait(barrier, NDEV - 1)

    def start_adm():
        for i in range(1, NOWN):
            peer = lax.rem(dp + i, NOWN)
            remote(adm_ref.at[peer], adm_in.at[dp], sems(adm_sem, 0), (peer, tab)).start()
            remote(alab_ref.at[peer], alab_in.at[dp], sems(adm_sem, 1), (peer, tab)).start()
        adm_in[dp] = adm_ref[dp]
        alab_in[dp] = alab_ref[dp]

    def wait_all(src, dst, array, at):
        pltpu.make_async_copy(src, src, array.at[(0,) + at]).wait()
        pltpu.make_async_copy(dst, dst, array.at[(1,) + at]).wait()

    def sum_adm():
        wait_all(adm_ref.at[0:7], adm_in.at[0:7], adm_sem, (0,))
        wait_all(alab_ref.at[0:7], alab_in.at[0:7], adm_sem, (1,))

        def put(at, value):
            for j in range(2):
                osum[at // 128 + j] = value[j * 128 : j * 128 + 128].astype(BF16)

        marks = jnp.concatenate([alab_in[o] for o in range(NOWN)], axis=0)
        sum_rows(marks, lambda i, j: i * 3 + j, lambda i: adm_in[i].astype(F32), OWN_ROWS, put)

        @pl.loop(1, 16)
        def _(i):
            peer = lax.rem(tab + i, 16)
            remote(osum.at[peer], osum_in.at[tab], sems(tab_sem), (dp, peer)).start()

        osum_in[tab] = osum[tab]

    def finish_adm():
        wait_all(osum.at[0:15], osum_in.at[0:15], tab_sem, ())
        total = osum_in[0].astype(F32)
        for j in range(1, 16):
            total = total + osum_in[j].astype(F32)
        agrad_ref[...] = total

    def start_qr(first, count):
        @pl.loop(first, first + count)
        def _(i):
            peer = lax.rem(me + i, NDEV)
            device = (lax.div(peer, 16), lax.rem(peer, 16))
            remote(qr_ref.at[peer], qr_in.at[me], sems(qr_sem, 0), device).start()
            remote(qlab_ref.at[peer], qlab_in.at[me], sems(qr_sem, 1), device).start()

    sent = [1]

    def gap(k):
        if k in fillers:
            fillers[k]()
        if GAPS[k]:
            start_qr(sent[0], GAPS[k])
            sent[0] += GAPS[k]

    bias_slots = ((0, 4, x), (4, 4, y), (8, 4, z))

    def bias_start(k):
        first, count, mine = bias_slots[k]
        slot = first + mine
        for i in range(1, count):
            device = beside(k, i)
            remote(bsum.at[slot], bsum.at[slot], sems(b_sem, first + i), device).start()

    def bias_wait(k):
        first, count, mine = bias_slots[k]
        for i in range(1, count):
            pltpu.make_async_copy(bsum.at[first], bsum.at[first], b_sem.at[0, first + i]).wait()
            pltpu.make_async_copy(bsum.at[first], bsum.at[first], b_sem.at[1, first + i]).wait()
        total = bsum[first]
        for i in range(1, count):
            total = total + bsum[first + i]
        return total

    theirs = pl.ds(pl.multiple_of((1 - core) * HALF, 128), HALF)
    pair = [
        remote(feat_ref.at[:, theirs], feat_in, sems(pair_sem, 0), partner),
        remote(dpre_ref, dpre_in, sems(pair_sem, 1), partner),
    ]
    for copy in pair:
        copy.start()
    for i in range(F // 2):
        part = lax.dot_general(
            dpre_ref[...], w_ref[i * 256 : (i + 1) * 256, :], (((1,), (1,)), ((), ())), preferred_element_type=F32
        )
        look[2 * i] = part[:, :E]
        look[2 * i + 1] = part[:, E:]
    for copy in pair:
        copy.wait()
    both = jnp.concatenate([dpre_ref[...], dpre_in[...]], axis=0)
    for i in range(HALF // 256):
        at = pl.multiple_of(core * HALF + i * 256, 256)
        feats = jnp.concatenate([feat_ref[:, pl.ds(at, 256)], feat_in[:, i * 256 : i * 256 + 256]], axis=0)
        block = lax.dot_general(feats, both, (((0,), (0,)), ((), ())), preferred_element_type=F32)
        for k in range(HID // 128):
            data[k * HALF + i * 256 : k * HALF + i * 256 + 256, :] = block[:, k * 128 : k * 128 + 128]
    bias = jnp.sum(dpre_ref[...].astype(F32), axis=0, keepdims=True) + jnp.sum(
        dpre_in[...].astype(F32), axis=0, keepdims=True
    )
    bsum[x] = jnp.concatenate([bias[:, k * 128 : k * 128 + 128] for k in range(HID // 128)], axis=0)

    def make_adm():
        bucket_adm(fields, adm_ref, alab_ref, look)
        start_adm()

    def make_q():
        bucket_plain(fields, 0, qr_ref, qlab_ref, look)

    def make_r():
        bucket_plain(fields, 1, qr_ref, qlab_ref, look)
        qr_in[me] = qr_ref[me]
        qlab_in[me] = qlab_ref[me]

    def sum_plain(t, out_ref):
        def put(at, value):
            out_ref[at : at + 256, :] = value

        marks = flat_marks(qlab_in[:, 0, :])[t]
        sum_rows(
            jnp.concatenate([marks[:, j * 128 : j * 128 + 128] for j in range(3)], axis=0),
            lambda i, j: j * 8 + i,
            lambda i: qr_in[i * 16 : i * 16 + 16, t].astype(F32).reshape(384, E),
            QROWS_DEV,
            put,
        )

    def sum_q():
        wait_all(qr_ref.at[0 : NDEV - 1], qr_in.at[0 : NDEV - 1], qr_sem, (0,))
        wait_all(qlab_ref.at[0 : NDEV - 1], qlab_in.at[0 : NDEV - 1], qr_sem, (1,))
        sum_plain(0, q_ref)

    def sum_r():
        sum_plain(1, r_ref)

    first_row = [pl.multiple_of(jnp.int32(0) + STREAMS[k][1], 16) for k in range(3)]
    starts = [[], [], []]
    gap_at = 0
    fillers = {0: make_adm, 1: make_q, 2: make_r, 4: sum_adm, 8: finish_adm, 10: sum_q, 11: sum_r}
    for stage in range(3):
        copies = []
        for k in range(3):
            n, p = piece(k, stage), place[STREAMS[k][2][stage]]
            axis, h, at, cur = STREAMS[k][2][stage], piece(k, stage) // 2, ROWS_AT[stage, k], first_row[k]
            far = data[pl.ds(pl.multiple_of(cur + turn(p, 2) * n, 16), n), :].astype(BF16)
            sbuf[at : at + n, :] = far
            for d, step in ((0, 1), (1, -1)):
                part = slice(at + d * h, at + d * h + h)
                copies.append(remote(sbuf.at[part], rbuf.at[part], sems(rs_sem, stage, k, d), beside(axis, step)))
                copies[-1].start()
        if stage == 0:
            bias_start(0)
        gap(gap_at)
        gap_at += 1
        for copy in copies:
            copy.wait()
        copies = []
        for k in range(3):
            n, p = piece(k, stage), place[STREAMS[k][2][stage]]
            axis, h, at, cur = STREAMS[k][2][stage], piece(k, stage) // 2, ROWS_AT[stage, k], first_row[k]
            for d, step in ((0, 1), (1, -1)):
                row = pl.multiple_of(cur + turn(p, step) * n, 16)
                to = at + n + d * n
                for e in range(2):
                    value = data[pl.ds(row + e * h, h), :]
                    if e == d:
                        value = value + rbuf[at + d * h : at + d * h + h, :].astype(F32)
                    sbuf[to + e * h : to + e * h + h, :] = value.astype(BF16)
                part = slice(to, to + n)
                copies.append(remote(sbuf.at[part], rbuf.at[part], sems(rs_sem, stage, k, 2 + d), beside(axis, step)))
                copies[-1].start()
        gap(gap_at)
        gap_at += 1
        for copy in copies:
            copy.wait()
        total = bias_wait(stage)
        if stage < 2:
            bsum[bias_slots[stage + 1][0] + bias_slots[stage + 1][2]] = total
            bias_start(stage + 1)
        else:
            bout_ref[...] = total
        for k in range(3):
            n, p = piece(k, stage), place[STREAMS[k][2][stage]]
            at, cur = ROWS_AT[stage, k], first_row[k]
            mine = pl.multiple_of(cur + p * n, 16)
            value = data[pl.ds(mine, n), :]
            value = value + rbuf[at + n : at + 2 * n, :].astype(F32) + rbuf[at + 2 * n : at + 3 * n, :].astype(F32)
            if stage < 2:
                data[pl.ds(mine, n), :] = value
            else:
                full_ref[core, pl.ds(mine, n), :] = value.astype(BF16)
            starts[k].append(cur)
            first_row[k] = mine

    forwards = []

    def forward(k, which, row, n):
        rows = pl.ds(pl.multiple_of(row, 16), n)
        forwards.append(
            remote(full_ref.at[core, rows], full_ref.at[core, rows], sems(fw_sem, k, which), partner)
        )
        forwards[-1].start()

    for stage in (2, 1, 0):
        copies = []
        for k in range(3):
            n, axis = piece(k, stage), STREAMS[k][2][stage]
            p, cur = place[axis], starts[k][stage]
            rows = pl.ds(pl.multiple_of(cur + p * n, 16), n)
            for d, step in ((0, 1), (1, -1)):
                copies.append(
                    remote(full_ref.at[core, rows], full_ref.at[core, rows], sems(ag_sem, stage, k, d), beside(axis, step))
                )
                copies[-1].start()
            if stage == 0:
                forward(k, 0, cur + p * n, n)
        gap(gap_at)
        gap_at += 1
        for copy in copies:
            copy.wait()
        copies = []
        for k in range(3):
            n, axis = piece(k, stage), STREAMS[k][2][stage]
            p, cur, h = place[axis], starts[k][stage], piece(k, stage) // 2
            for d, step in ((0, 1), (1, -1)):
                rows = pl.ds(pl.multiple_of(cur + turn(p, -step) * n + d * h, 8), h)
                copies.append(
                    remote(
                        full_ref.at[core, rows], full_ref.at[core, rows], sems(ag_sem, stage, k, 2 + d), beside(axis, step)
                    )
                )
                copies[-1].start()
            if stage == 0:
                forward(k, 1, cur + turn(p, 1) * n, n)
                forward(k, 2, cur + turn(p, -1) * n, n)
        gap(gap_at)
        gap_at += 1
        for copy in copies:
            copy.wait()
        if stage == 0:
            for k in range(3):
                n = piece(k, 0)
                forward(k, 3, starts[k][0] + turn(place[STREAMS[k][2][0]], 2) * n, n)
    for copy in forwards:
        copy.wait()


def widen_kernel(full_ref, w_ref):
    for k in range(HID // 128):
        w_ref[:, k * 128 : k * 128 + 128] = full_ref[0, k].astype(F32)


def spec():
    return pl.BlockSpec(memory_space=VMEM)


def shape(dims, dtype):
    return jax.ShapeDtypeStruct(dims, dtype)


def local(features, w_first, b_first, grad_out, admit, owner, adm_row, q_shard, q_local, r_shard, r_local):
    fields = [
        f.T if f.ndim == 2 else f.transpose(1, 2, 0)
        for f in (admit, owner, adm_row, q_shard, q_local, r_shard, r_local)
    ]
    dma = pltpu.SemaphoreType.DMA
    full, b_sum, adm_grad, q_grad, r_grad = pl.pallas_call(
        step_kernel,
        out_shape=(
            shape((2, HALF_ROWS, 128), BF16),
            shape((8, 128), F32),
            shape((128, E), F32),
            shape((QROWS_DEV, E), F32),
            shape((QROWS_DEV, E), F32),
        ),
        in_specs=[spec()] * 11,
        out_specs=tuple([spec()] * 5),
        scratch_shapes=[
            VMEM((SAMP, HALF), BF16),
            VMEM((SAMP, HID), BF16),
            VMEM((SAMP, HID), BF16),
            VMEM((HALF_ROWS, 128), F32),
            VMEM((F, SAMP, E), F32),
            VMEM((ROWS_ALL, 128), BF16),
            VMEM((ROWS_ALL, 128), BF16),
            VMEM((12, 8, 128), F32),
            VMEM((NDEV, 2, QCAP, E), BF16),
            VMEM((NDEV, 2, QCAP, E), BF16),
            VMEM((NDEV, 1, 128), F32),
            VMEM((NDEV, 1, 128), F32),
            VMEM((NOWN, CAP, E), BF16),
            VMEM((NOWN, CAP, E), BF16),
            VMEM((NOWN, 3, 128), F32),
            VMEM((NOWN, 3, 128), F32),
            VMEM((16, 128, E), BF16),
            VMEM((16, 128, E), BF16),
            dma((2, 2)),
            dma((2, 3, 3, 4)),
            dma((2, 3, 3, 4)),
            dma((2, 3, 4)),
            dma((2, 12)),
            dma((2, 2)),
            dma((2, 2)),
            dma((2,)),
        ],
        compiler_params=pltpu.CompilerParams(vmem_limit_bytes=60 << 20, collective_id=0, has_side_effects=True),
        name="step",
    )(features, w_first, b_first.reshape(1, HID), grad_out, *fields)
    w_grad = pl.pallas_call(
        widen_kernel,
        grid=(8,),
        out_shape=shape((WROWS, HID), F32),
        in_specs=[pl.BlockSpec((1, 8, 256, 128), lambda i: (i // 4, 0, i % 4, 0))],
        out_specs=pl.BlockSpec((256, HID), lambda i: (i, 0)),
        name="widen",
    )(full.reshape(2, 8, HALF, 128))
    return (w_grad, b_sum.reshape(HID), adm_grad, q_grad, r_grad)


def solution(mesh):
    both = ("dp", "table")
    two, three = P(both, None), P(both, None, None)
    return jax.shard_map(
        local,
        mesh=mesh,
        in_specs=(two, P(), P(), two, two, three, two, three, two, three, two),
        out_specs=(P(), P(), two, two, two),
        check_vma=False,
    )
```

```python
import functools

import jax
import jax.numpy as jnp
from jax import lax
from jax.experimental import pallas as pl
from jax.experimental.pallas import tpu as pltpu
from jax.sharding import PartitionSpec as P

E = 128
F = 16
SAMP = 128
HID = 1024
WROWS = 2048
QCAP = 24
CAP = 384
NDEV = 128
NOWN = 8
QROWS_DEV = 4096
OWN_ROWS = 2048
SLOTS = 3072
HALF = 1024
HALF_ROWS = 8192
F32 = jnp.float32
BF16 = jnp.bfloat16
VMEM = pltpu.VMEM


def iota(shape, dim):
    return lax.broadcasted_iota(jnp.int32, shape, dim)


def onehot(cond):
    return jnp.where(cond, 1.0, 0.0).astype(BF16)


def ranks_of(dest_t, n_dest, ramp):
    hits = [onehot(iota((n_dest, SAMP), 0) == dest_t[f : f + 1, :]) for f in range(F)]
    stacked = jnp.concatenate(hits, axis=0)
    counts = jnp.dot(stacked, ramp, preferred_element_type=F32)
    base = jnp.zeros((n_dest, SAMP), F32)
    rows = []
    for f in range(F):
        part = counts[f * n_dest : (f + 1) * n_dest]
        before = part[:, :SAMP] + base
        rows.append(jnp.sum(before * hits[f].astype(F32), axis=0, keepdims=True))
        base = base + part[:, SAMP:]
    return jnp.concatenate(rows, axis=0), hits


def fields_of(fields):
    field_t = [ref[...] if len(ref.shape) == 2 else ref[:, 0, :] for ref in fields]
    stacked = jnp.concatenate([t.astype(F32) for t in field_t] + [jnp.zeros((F, SAMP), F32)], axis=0)
    return field_t, jnp.transpose(stacked).astype(jnp.int32)


def ramp_of():
    return jnp.concatenate(
        [onehot(iota((SAMP, SAMP), 0) < iota((SAMP, SAMP), 1)), jnp.ones((SAMP, SAMP), BF16)], axis=1
    )


def as_columns(rank_t):
    return jnp.transpose(jnp.concatenate([rank_t, jnp.zeros((SAMP - F, SAMP), F32)], axis=0)).astype(jnp.int32)


def fill(look, slot_t, half_of, store):
    rhs = []
    for f in range(F):
        half = half_of(f)
        value = look[f]
        rhs.append(
            jnp.concatenate(
                [jnp.where(half == 0, value, 0.0).astype(BF16), jnp.where(half == 1, value, 0.0).astype(BF16)],
                axis=1,
            )
        )
    rhs = jnp.concatenate(rhs, axis=0)
    for m in range(8):
        want = iota((192, SAMP), 0) + m * 192
        picked = jnp.concatenate([onehot(want == slot_t[f : f + 1, :]) for f in range(F)], axis=1)
        out = jnp.dot(picked, rhs, preferred_element_type=F32)
        store(m, 0, out[:, :E])
        store(m, 1, out[:, E:])


def bucket_adm(fields, adm_ref, alab_ref, look):
    field_t, col = fields_of(fields)

    def field(t, f):
        return col[:, t * F + f : t * F + f + 1]

    dest = jnp.where(field_t[0] == 1, field_t[1], -1)
    rank_t, _ = ranks_of(dest, 16, ramp_of())
    rank_col = as_columns(rank_t)
    lane = iota((SAMP, 128), 1)
    parts = []
    for f in range(F):
        mark = field(2, f) + 1
        hit = (lane == rank_col[:, f : f + 1] % 128) & (field(0, f) == 1)
        parts.append(
            jnp.concatenate(
                [
                    jnp.where(hit, mark // 64, 0).astype(F32).astype(BF16),
                    jnp.where(hit, mark % 64, 0).astype(F32).astype(BF16),
                ],
                axis=1,
            )
        )
    rank = rank_t.astype(jnp.int32)
    code = jnp.where(dest >= 0, dest * 3 + rank // 128, -1)
    codes = jnp.concatenate([onehot(iota((32, SAMP), 0) == code[f : f + 1, :]) for f in range(F)], axis=1)
    alab = jnp.dot(codes, jnp.concatenate(parts, axis=0), preferred_element_type=F32)
    alab = alab[:, :128] * 64.0 + alab[:, 128:]
    for o in range(NOWN):
        alab_ref[o] = alab[o * 3 : o * 3 + 3, :]

    def store(m, h, value):
        adm_ref[h * 4 + m // 2, (m % 2) * 192 : (m % 2) * 192 + 192, :] = value.astype(BF16)

    fill(
        look,
        jnp.where(dest >= 0, (dest % 4) * CAP + rank, -1),
        lambda f: jnp.where(field(0, f) == 1, field(1, f) // 4, -1),
        store,
    )


def bucket_plain(fields, table, qr_ref, lab_ref, look):
    field_t, col = fields_of(fields)

    def field(t, f):
        return col[:, t * F + f : t * F + f + 1]

    shard, row, at = 3 + 2 * table, 4 + 2 * table, 64 * table
    dest = jnp.where(field_t[0] == 0, field_t[shard], -1)
    rank_t, hits = ranks_of(dest, NDEV, ramp_of())
    rank_col = as_columns(rank_t)
    lane = iota((SAMP, 128), 1)
    parts = []
    for f in range(F):
        mark = field(row, f) + 1
        rank = rank_col[:, f : f + 1]
        value = jnp.where(lane < at + 32, mark // 64, mark % 64)
        hit = ((lane - at == rank) | (lane - at - 32 == rank)) & (field(0, f) == 0)
        parts.append(jnp.where(hit, value, 0).astype(F32).astype(BF16))
    lab = jnp.dot(jnp.concatenate(hits, axis=1), jnp.concatenate(parts, axis=0), preferred_element_type=F32)
    lab = lab.reshape(lab_ref.shape)
    lab_ref[...] = lab if table == 0 else lab_ref[...] + lab

    def store(m, h, value):
        qr_ref[h * 64 + m * 8 : h * 64 + m * 8 + 8, table] = value.reshape(8, QCAP, E).astype(BF16)

    fill(
        look,
        jnp.where(dest >= 0, (dest % 64) * QCAP + rank_t.astype(jnp.int32), -1),
        lambda f: jnp.where(field(0, f) == 0, field(shard, f) // 64, -1),
        store,
    )


def flat_marks(lab):
    slot = iota((128, 1536), 1)
    inner = slot % 384
    spread = onehot(iota((128, 1536), 0) == (slot // 384) * 32 + inner % QCAP)
    wide = jnp.dot(lab.astype(BF16), spread, preferred_element_type=F32)
    wide = jnp.where(inner // QCAP == iota((128, 1536), 0) % 16, wide, 0.0).astype(BF16)
    gather = onehot(iota((16, 128), 0) == iota((16, 128), 1) // 16)
    flat = jnp.dot(gather, wide, preferred_element_type=F32)[:8]
    return [flat[:, t * 768 : t * 768 + 384] * 64.0 + flat[:, t * 768 + 384 : t * 768 + 768] for t in range(2)]


def sum_rows(marks, group, block, n_rows, put):
    hi_rows = n_rows // 4
    mark = marks.astype(jnp.int32) - 1
    low = jnp.where(mark >= 0, mark // hi_rows, -1)
    high = jnp.where(mark >= 0, mark % hi_rows, -1)
    low_col = jnp.transpose(
        jnp.concatenate([low.astype(F32), jnp.zeros((SAMP - 24, SAMP), F32)], axis=0)
    ).astype(jnp.int32)
    order = [group(i, j) for i in range(8) for j in range(3)]
    rhs = []
    for i in range(8):
        values = block(i)
        for j in range(3):
            g = group(i, j)
            v = values[j * 128 : (j + 1) * 128]
            which = low_col[:, g : g + 1]
            rhs.append(jnp.concatenate([jnp.where(which == k, v, 0.0).astype(BF16) for k in range(4)], axis=1))
    rhs = jnp.concatenate(rhs, axis=0)
    for m in range(hi_rows // 256):
        want = iota((256, SAMP), 0) + m * 256
        picked = jnp.concatenate([onehot(want == high[g : g + 1, :]) for g in order], axis=1)
        out = jnp.dot(picked, rhs, preferred_element_type=F32)
        for k in range(4):
            put(k * hi_rows + m * 256, out[:, k * E : (k + 1) * E])


MESH = pl.DeviceIdType.MESH
STREAMS = ((3072, 0, (1, 2, 0)), (3072, 3072, (2, 0, 1)), (2048, 6144, (0, 1, 2)))


def piece(stream, stage):
    return STREAMS[stream][0] // 4 ** (stage + 1)


def stage_rows():
    table, at = {}, 0
    for stage in range(3):
        for stream in range(3):
            table[stage, stream] = at
            at += 3 * piece(stream, stage)
    return table, at


ROWS_AT, ROWS_ALL = stage_rows()
GAPS = (0, 42, 30, 25, 20, 10, 0, 0, 0, 0)


def step_kernel(
    feat_hbm, w_hbm, b_hbm, g_hbm, h0, h1, h2, h3, h4, h5, h6,
    full_ref, bout_ref, agrad_ref, q_ref, r_ref,
    feat_ref, w_ref, b_ref, g_ref, f0, f1, f2, f3, f4, f5, f6, in_sem,
    feat_in, dpre_ref, dpre_in, data, look, sbuf, rbuf, bsum,
    qr_ref, qr_in, qlab_ref, qlab_in, adm_ref, adm_in, alab_ref, alab_in, osum, osum_in,
    pair_sem, rs_sem, ag_sem, fw_sem, b_sem, adm_sem, qr_sem, tab_sem,
):
    dp, tab = lax.axis_index("dp"), lax.axis_index("table")
    core, x = lax.rem(dp, 2), lax.div(dp, 2)
    y, z = lax.div(tab, 4), lax.rem(tab, 4)
    me = dp * 16 + tab
    place = (x, y, z)

    def turn(value, step):
        return lax.rem(value + step + 4, 4)

    def beside(axis, step):
        if axis == 0:
            return (turn(x, step) * 2 + core, tab)
        if axis == 1:
            return (dp, turn(y, step) * 4 + z)
        return (dp, y * 4 + turn(z, step))

    partner = (dp + 1 - 2 * core, tab)

    def remote(src, dst, sems, device):
        return pltpu.make_async_remote_copy(
            src_ref=src, dst_ref=dst, send_sem=sems[0], recv_sem=sems[1], device_id=device, device_id_type=MESH
        )

    def sems(array, *at):
        return array.at[(0,) + at], array.at[(1,) + at]

    def load(i, src, dst):
        copy = pltpu.make_async_copy(src, dst, in_sem.at[i])
        copy.start()
        return copy

    feat_load = load(0, feat_hbm, feat_ref)
    w_loads = [load(1 + i, w_hbm.at[pl.ds(i * 512, 512)], w_ref.at[pl.ds(i * 512, 512)]) for i in range(4)]
    late_loads = [load(5, b_hbm, b_ref), load(6, g_hbm, g_ref)]
    held = (h0, h1, h2, h3, h4, h5, h6)
    fields = (f0, f1, f2, f3, f4, f5, f6)
    field_loads = [load(7 + i, held[i], fields[i]) for i in range(7)]

    barrier = pltpu.get_barrier_semaphore()

    @pl.loop(1, NDEV)
    def _(i):
        peer = lax.rem(me + i, NDEV)
        pl.semaphore_signal(
            barrier, inc=1, device_id=(lax.div(peer, 16), lax.rem(peer, 16)), device_id_type=MESH
        )

    feat_load.wait()
    pre = jnp.zeros((SAMP, HID), F32)
    for i in range(4):
        w_loads[i].wait()
        pre = pre + jnp.dot(
            feat_ref[:, i * 512 : i * 512 + 512], w_ref[i * 512 : i * 512 + 512, :], preferred_element_type=F32
        )
    for copy in late_loads:
        copy.wait()
    pre = pre + b_ref[...]
    sig = 1.0 / (1.0 + jnp.exp(-pre))
    dpre_ref[...] = (g_ref[...].astype(F32) * sig * (1.0 + pre * (1.0 - sig))).astype(BF16)
    pl.semaphore_wait(barrier, NDEV - 1)

    def start_adm():
        for i in range(1, NOWN):
            peer = lax.rem(dp + i, NOWN)
            remote(adm_ref.at[peer], adm_in.at[dp], sems(adm_sem, 0), (peer, tab)).start()
            remote(alab_ref.at[peer], alab_in.at[dp], sems(adm_sem, 1), (peer, tab)).start()
        adm_in[dp] = adm_ref[dp]
        alab_in[dp] = alab_ref[dp]

    def wait_all(src, dst, array, at):
        pltpu.make_async_copy(src, src, array.at[(0,) + at]).wait()
        pltpu.make_async_copy(dst, dst, array.at[(1,) + at]).wait()

    def sum_adm():
        wait_all(adm_ref.at[0:7], adm_in.at[0:7], adm_sem, (0,))
        wait_all(alab_ref.at[0:7], alab_in.at[0:7], adm_sem, (1,))

        def put(at, value):
            for j in range(2):
                osum[at // 128 + j] = value[j * 128 : j * 128 + 128].astype(BF16)

        marks = jnp.concatenate([alab_in[o] for o in range(NOWN)], axis=0)
        sum_rows(marks, lambda i, j: i * 3 + j, lambda i: adm_in[i].astype(F32), OWN_ROWS, put)

        @pl.loop(1, 16)
        def _(i):
            peer = lax.rem(tab + i * 7, 16)
            remote(osum.at[peer], osum_in.at[tab], sems(tab_sem), (dp, peer)).start()

        osum_in[tab] = osum[tab]

    def finish_adm():
        wait_all(osum.at[0:15], osum_in.at[0:15], tab_sem, ())
        total = osum_in[0].astype(F32)
        for j in range(1, 16):
            total = total + osum_in[j].astype(F32)
        agrad_ref[...] = total

    def start_qr(first, count):
        @pl.loop(first, first + count)
        def _(i):
            peer = lax.rem(me + i * 37, NDEV)
            device = (lax.div(peer, 16), lax.rem(peer, 16))
            remote(qr_ref.at[peer], qr_in.at[me], sems(qr_sem, 0), device).start()
            remote(qlab_ref.at[peer], qlab_in.at[me], sems(qr_sem, 1), device).start()

    sent = [1]

    def gap(k):
        for work in before.get(k, ()):
            work()
        if GAPS[k]:
            start_qr(sent[0], GAPS[k])
            sent[0] += GAPS[k]
        for work in after.get(k, ()):
            work()

    bias_slots = ((0, 4, x), (4, 4, y), (8, 4, z))

    def bias_start(k):
        first, count, mine = bias_slots[k]
        slot = first + mine
        for i in range(1, count):
            device = beside(k, i)
            remote(bsum.at[slot], bsum.at[slot], sems(b_sem, first + i), device).start()

    def bias_wait(k):
        first, count, mine = bias_slots[k]
        for i in range(1, count):
            pltpu.make_async_copy(bsum.at[first], bsum.at[first], b_sem.at[0, first + i]).wait()
            pltpu.make_async_copy(bsum.at[first], bsum.at[first], b_sem.at[1, first + i]).wait()
        total = bsum[first]
        for i in range(1, count):
            total = total + bsum[first + i]
        return total

    theirs = pl.ds(pl.multiple_of((1 - core) * HALF, 128), HALF)
    pair = [
        remote(feat_ref.at[:, theirs], feat_in, sems(pair_sem, 0), partner),
        remote(dpre_ref, dpre_in, sems(pair_sem, 1), partner),
    ]
    for copy in pair:
        copy.start()
    for i in range(F // 2):
        part = lax.dot_general(
            dpre_ref[...], w_ref[i * 256 : (i + 1) * 256, :], (((1,), (1,)), ((), ())), preferred_element_type=F32
        )
        look[2 * i] = part[:, :E]
        look[2 * i + 1] = part[:, E:]
    for copy in pair:
        copy.wait()
    both = jnp.concatenate([dpre_ref[...], dpre_in[...]], axis=0)
    bias = jnp.sum(dpre_ref[...].astype(F32), axis=0, keepdims=True) + jnp.sum(
        dpre_in[...].astype(F32), axis=0, keepdims=True
    )
    bsum[x] = jnp.concatenate([bias[:, k * 128 : k * 128 + 128] for k in range(HID // 128)], axis=0)

    def make_adm():
        for copy in field_loads:
            copy.wait()
        bucket_adm(fields, adm_ref, alab_ref, look)
        start_adm()

    def make_q():
        bucket_plain(fields, 0, qr_ref, qlab_ref, look)

    def make_r():
        bucket_plain(fields, 1, qr_ref, qlab_ref, look)
        qr_in[me] = qr_ref[me]
        qlab_in[me] = qlab_ref[me]

    def sum_plain(t, out_ref):
        def put(at, value):
            out_ref[at : at + 256, :] = value

        marks = flat_marks(qlab_in[:, 0, :])[t]
        sum_rows(
            jnp.concatenate([marks[:, j * 128 : j * 128 + 128] for j in range(3)], axis=0),
            lambda i, j: j * 8 + i,
            lambda i: qr_in[i * 16 : i * 16 + 16, t].astype(F32).reshape(384, E),
            QROWS_DEV,
            put,
        )

    def sum_q():
        wait_all(qr_ref.at[0 : NDEV - 1], qr_in.at[0 : NDEV - 1], qr_sem, (0,))
        wait_all(qlab_ref.at[0 : NDEV - 1], qlab_in.at[0 : NDEV - 1], qr_sem, (1,))
        sum_plain(0, q_ref)

    def sum_r():
        sum_plain(1, r_ref)

    def half_block(k):
        rows, first, _ = STREAMS[k]
        col, width = first // HALF * 128, rows // HALF * 128
        for i in range(HALF // 256):
            at = pl.multiple_of(core * HALF + i * 256, 256)
            feats = jnp.concatenate([feat_ref[:, pl.ds(at, 256)], feat_in[:, i * 256 : i * 256 + 256]], axis=0)
            block = lax.dot_general(
                feats, both[:, col : col + width], (((0,), (0,)), ((), ())), preferred_element_type=F32
            )
            for j in range(width // 128):
                to = first + j * HALF + i * 256
                data[to : to + 256, :] = block[:, j * 128 : j * 128 + 128]

    first_row = [pl.multiple_of(jnp.int32(0) + STREAMS[k][1], 16) for k in range(3)]
    starts = [[], [], []]
    flying = [[], [], []]

    def send(k, *copy):
        flying[k].append(remote(*copy))
        flying[k][-1].start()

    def land(k):
        for copy in flying[k]:
            copy.wait()
        flying[k] = []

    def where_at(k, stage):
        axis = STREAMS[k][2][stage]
        return piece(k, stage), axis, place[axis], ROWS_AT[stage, k]

    def reduce_far(stage, k):
        n, axis, p, at = where_at(k, stage)
        h, cur = n // 2, first_row[k]
        sbuf[at : at + n, :] = data[pl.ds(pl.multiple_of(cur + turn(p, 2) * n, 16), n), :].astype(BF16)
        for d, step in ((0, 1), (1, -1)):
            part = slice(at + d * h, at + d * h + h)
            send(k, sbuf.at[part], rbuf.at[part], sems(rs_sem, stage, k, d), beside(axis, step))

    def reduce_near(stage, k):
        n, axis, p, at = where_at(k, stage)
        h, cur = n // 2, first_row[k]
        land(k)
        for d, step in ((0, 1), (1, -1)):
            row = pl.multiple_of(cur + turn(p, step) * n, 16)
            to = at + n + d * n
            for e in range(2):
                value = data[pl.ds(row + e * h, h), :]
                if e == d:
                    value = value + rbuf[at + d * h : at + d * h + h, :].astype(F32)
                sbuf[to + e * h : to + e * h + h, :] = value.astype(BF16)
            part = slice(to, to + n)
            send(k, sbuf.at[part], rbuf.at[part], sems(rs_sem, stage, k, 2 + d), beside(axis, step))

    def reduce_end(stage, k):
        n, axis, p, at = where_at(k, stage)
        cur = first_row[k]
        land(k)
        mine = pl.multiple_of(cur + p * n, 16)
        value = data[pl.ds(mine, n), :]
        value = value + rbuf[at + n : at + 2 * n, :].astype(F32) + rbuf[at + 2 * n : at + 3 * n, :].astype(F32)
        data[pl.ds(mine, n), :] = value
        starts[k].append(cur)
        first_row[k] = mine

    def last_send(k):
        n, axis, p, at = where_at(k, 2)
        for i in range(1, 4):
            part = slice(at + (i - 1) * n, at + i * n)
            row = pl.multiple_of(first_row[k] + turn(p, i) * n, 16)
            sbuf[part, :] = data[pl.ds(row, n), :].astype(BF16)
            send(k, sbuf.at[part], rbuf.at[part], sems(rs_sem, 2, k, i - 1), beside(axis, i))

    def last_end(k):
        n, axis, p, at = where_at(k, 2)
        land(k)
        rows = pl.ds(pl.multiple_of(first_row[k] + p * n, 16), n)
        value = data[rows, :]
        for i in range(3):
            value = value + rbuf[at + i * n : at + i * n + n, :].astype(F32)
        full_ref[core, rows, :] = value.astype(BF16)
        for i in range(1, 4):
            spread(k, rows, sems(ag_sem, 2, k, i - 1), beside(axis, i))

    def spread(k, rows, pair_of, device):
        send(k, full_ref.at[core, rows], full_ref.at[core, rows], pair_of, device)

    def gather_near(stage, k):
        n, axis, p, _ = where_at(k, stage)
        land(k)
        rows = pl.ds(pl.multiple_of(starts[k][stage] + p * n, 16), n)
        for d, step in ((0, 1), (1, -1)):
            spread(k, rows, sems(ag_sem, stage, k, d), beside(axis, step))

    def gather_far(stage, k):
        n, axis, p, _ = where_at(k, stage)
        h = n // 2
        land(k)
        for d, step in ((0, 1), (1, -1)):
            rows = pl.ds(pl.multiple_of(starts[k][stage] + turn(p, -step) * n + d * h, 8), h)
            spread(k, rows, sems(ag_sem, stage, k, 2 + d), beside(axis, step))

    forwards = []

    def forward(k, which, step):
        n, _, p, _ = where_at(k, 0)
        rows = pl.ds(pl.multiple_of(starts[k][0] + turn(p, step) * n, 16), n)
        forwards.append(
            remote(full_ref.at[core, rows], full_ref.at[core, rows], sems(fw_sem, k, which), partner)
        )
        forwards[-1].start()

    def bias_turn(stage):
        total = bias_wait(stage)
        if stage == 2:
            bout_ref[...] = total
        else:
            first, _, mine = bias_slots[stage + 1]
            bsum[first + mine] = total
            bias_start(stage + 1)

    before = {0: (make_adm,), 1: (make_q, make_r)}
    after = {4: (sum_adm,), 7: (finish_adm,), 8: (sum_q,), 9: (sum_r,)}

    bias_start(0)
    for k in range(3):
        half_block(k)
        reduce_far(0, k)
    gap(0)
    for k in range(3):
        reduce_near(0, k)
    gap(1)
    for k in range(3):
        reduce_end(0, k)
        reduce_far(1, k)
    bias_turn(0)
    gap(2)
    for k in range(3):
        reduce_near(1, k)
    gap(3)
    for k in range(3):
        reduce_end(1, k)
        last_send(k)
    bias_turn(1)
    gap(4)
    for k in range(3):
        last_end(k)
    bias_turn(2)
    gap(5)
    for k in range(3):
        gather_near(1, k)
    gap(6)
    for k in range(3):
        gather_far(1, k)
    gap(7)
    for k in range(3):
        gather_near(0, k)
        forward(k, 0, 0)
    gap(8)
    for k in range(3):
        gather_far(0, k)
        forward(k, 1, 1)
        forward(k, 2, -1)
    gap(9)
    for k in range(3):
        land(k)
        forward(k, 3, 2)
    for copy in forwards:
        copy.wait()


def finish_kernel(full_ref, q_ref, r_ref, a_ref, b_ref, w_out, q_out, r_out, a_out, b_out, wide, sem):
    stores = []

    def store(src, dst):
        stores.append(pltpu.make_async_copy(src, dst, sem.at[len(stores)]))
        stores[-1].start()

    store(q_ref, q_out)
    store(r_ref, r_out)
    for i in range(8):
        for k in range(HID // 128):
            value = full_ref[i // 4, k, i % 4 * 256 : i % 4 * 256 + 256, :]
            wide[i * 256 : i * 256 + 256, k * 128 : k * 128 + 128] = value.astype(F32)
        store(wide.at[i * 256 : i * 256 + 256], w_out.at[i * 256 : i * 256 + 256])
    store(a_ref, a_out)
    store(b_ref, b_out)
    for copy in stores:
        copy.wait()


def spec():
    return pl.BlockSpec(memory_space=VMEM)


def shape(dims, dtype):
    return jax.ShapeDtypeStruct(dims, dtype)


def local(features, w_first, b_first, grad_out, admit, owner, adm_row, q_shard, q_local, r_shard, r_local):
    fields = [
        f.T if f.ndim == 2 else f.transpose(1, 2, 0)
        for f in (admit, owner, adm_row, q_shard, q_local, r_shard, r_local)
    ]
    dma = pltpu.SemaphoreType.DMA
    full, b_rows, a_rows, q_rows, r_rows = pl.pallas_call(
        step_kernel,
        out_shape=(
            shape((2, HALF_ROWS, 128), BF16),
            shape((8, 128), F32),
            shape((128, E), F32),
            shape((QROWS_DEV, E), F32),
            shape((QROWS_DEV, E), F32),
        ),
        in_specs=[pl.BlockSpec(memory_space=pltpu.HBM)] * 11,
        out_specs=tuple([spec()] * 5),
        scratch_shapes=[
            VMEM((SAMP, WROWS), BF16),
            VMEM((WROWS, HID), BF16),
            VMEM((1, HID), F32),
            VMEM((SAMP, HID), BF16),
            *[VMEM(f.shape, jnp.int32) for f in fields],
            dma((14,)),
            VMEM((SAMP, HALF), BF16),
            VMEM((SAMP, HID), BF16),
            VMEM((SAMP, HID), BF16),
            VMEM((HALF_ROWS, 128), F32),
            VMEM((F, SAMP, E), F32),
            VMEM((ROWS_ALL, 128), BF16),
            VMEM((ROWS_ALL, 128), BF16),
            VMEM((12, 8, 128), F32),
            VMEM((NDEV, 2, QCAP, E), BF16),
            VMEM((NDEV, 2, QCAP, E), BF16),
            VMEM((NDEV, 1, 128), F32),
            VMEM((NDEV, 1, 128), F32),
            VMEM((NOWN, CAP, E), BF16),
            VMEM((NOWN, CAP, E), BF16),
            VMEM((NOWN, 3, 128), F32),
            VMEM((NOWN, 3, 128), F32),
            VMEM((16, 128, E), BF16),
            VMEM((16, 128, E), BF16),
            dma((2, 2)),
            dma((2, 3, 3, 4)),
            dma((2, 3, 3, 4)),
            dma((2, 3, 4)),
            dma((2, 12)),
            dma((2, 2)),
            dma((2, 2)),
            dma((2,)),
        ],
        compiler_params=pltpu.CompilerParams(vmem_limit_bytes=44 << 20, collective_id=0, has_side_effects=True),
        name="step",
    )(*[pltpu.with_memory_space_constraint(v, pltpu.HBM) for v in (features, w_first, b_first.reshape(1, HID), grad_out, *fields)])
    w_grad, q_grad, r_grad, adm_grad, b_sum = pl.pallas_call(
        finish_kernel,
        out_shape=(
            shape((WROWS, HID), F32),
            shape((QROWS_DEV, E), F32),
            shape((QROWS_DEV, E), F32),
            shape((128, E), F32),
            shape((8, 128), F32),
        ),
        in_specs=[spec()] * 5,
        out_specs=tuple([pl.BlockSpec(memory_space=pltpu.HBM)] * 5),
        scratch_shapes=[VMEM((WROWS, HID), F32), dma((12,))],
        compiler_params=pltpu.CompilerParams(vmem_limit_bytes=20 << 20),
        name="finish",
    )(full.reshape(2, 8, HALF, 128), q_rows, r_rows, a_rows, b_rows)
    return (w_grad, b_sum.reshape(HID), adm_grad, q_grad, r_grad)


def solution(mesh):
    both = ("dp", "table")
    two, three = P(both, None), P(both, None, None)
    return jax.shard_map(
        local,
        mesh=mesh,
        in_specs=(two, P(), P(), two, two, three, two, three, two, three, two),
        out_specs=(P(), P(), two, two, two),
        check_vma=False,
    )
```

```python
import functools

import jax
import jax.numpy as jnp
from jax import lax
from jax.experimental import pallas as pl
from jax.experimental.pallas import tpu as pltpu
from jax.sharding import PartitionSpec as P

E = 128
F = 16
SAMP = 128
HID = 1024
WROWS = 2048
QCAP = 24
CAP = 384
NDEV = 128
NOWN = 8
QROWS_DEV = 4096
OWN_ROWS = 2048
SLOTS = 3072
HALF = 1024
HALF_ROWS = 8192
F32 = jnp.float32
BF16 = jnp.bfloat16
VMEM = pltpu.VMEM


def iota(shape, dim):
    return lax.broadcasted_iota(jnp.int32, shape, dim)


def onehot(cond):
    return jnp.where(cond, 1.0, 0.0).astype(BF16)


def ranks_of(dest_t, n_dest, ramp):
    hits = [onehot(iota((n_dest, SAMP), 0) == dest_t[f : f + 1, :]) for f in range(F)]
    stacked = jnp.concatenate(hits, axis=0)
    counts = jnp.dot(stacked, ramp, preferred_element_type=F32)
    base = jnp.zeros((n_dest, SAMP), F32)
    rows = []
    for f in range(F):
        part = counts[f * n_dest : (f + 1) * n_dest]
        before = part[:, :SAMP] + base
        rows.append(jnp.sum(before * hits[f].astype(F32), axis=0, keepdims=True))
        base = base + part[:, SAMP:]
    return jnp.concatenate(rows, axis=0), hits


def fields_of(fields):
    field_t = [ref[...] if len(ref.shape) == 2 else ref[:, 0, :] for ref in fields]
    stacked = jnp.concatenate([t.astype(F32) for t in field_t] + [jnp.zeros((F, SAMP), F32)], axis=0)
    return field_t, jnp.transpose(stacked).astype(jnp.int32)


def ramp_of():
    return jnp.concatenate(
        [onehot(iota((SAMP, SAMP), 0) < iota((SAMP, SAMP), 1)), jnp.ones((SAMP, SAMP), BF16)], axis=1
    )


def as_columns(rank_t):
    return jnp.transpose(jnp.concatenate([rank_t, jnp.zeros((SAMP - F, SAMP), F32)], axis=0)).astype(jnp.int32)


def fill(look, slot_t, half_of, store):
    rhs = []
    for f in range(F):
        half = half_of(f)
        value = look[f]
        rhs.append(
            jnp.concatenate(
                [jnp.where(half == 0, value, 0.0).astype(BF16), jnp.where(half == 1, value, 0.0).astype(BF16)],
                axis=1,
            )
        )
    rhs = jnp.concatenate(rhs, axis=0)
    for m in range(8):
        want = iota((192, SAMP), 0) + m * 192
        picked = jnp.concatenate([onehot(want == slot_t[f : f + 1, :]) for f in range(F)], axis=1)
        out = jnp.dot(picked, rhs, preferred_element_type=F32)
        store(m, 0, out[:, :E])
        store(m, 1, out[:, E:])


def bucket_adm(fields, adm_ref, alab_ref, look):
    field_t, col = fields_of(fields)

    def field(t, f):
        return col[:, t * F + f : t * F + f + 1]

    dest = jnp.where(field_t[0] == 1, field_t[1], -1)
    rank_t, _ = ranks_of(dest, 16, ramp_of())
    rank_col = as_columns(rank_t)
    lane = iota((SAMP, 128), 1)
    parts = []
    for f in range(F):
        mark = field(2, f) + 1
        hit = (lane == rank_col[:, f : f + 1] % 128) & (field(0, f) == 1)
        parts.append(
            jnp.concatenate(
                [
                    jnp.where(hit, mark // 64, 0).astype(F32).astype(BF16),
                    jnp.where(hit, mark % 64, 0).astype(F32).astype(BF16),
                ],
                axis=1,
            )
        )
    rank = rank_t.astype(jnp.int32)
    code = jnp.where(dest >= 0, dest * 3 + rank // 128, -1)
    codes = jnp.concatenate([onehot(iota((32, SAMP), 0) == code[f : f + 1, :]) for f in range(F)], axis=1)
    alab = jnp.dot(codes, jnp.concatenate(parts, axis=0), preferred_element_type=F32)
    alab = alab[:, :128] * 64.0 + alab[:, 128:]
    for o in range(NOWN):
        alab_ref[o] = alab[o * 3 : o * 3 + 3, :]

    def store(m, h, value):
        adm_ref[h * 4 + m // 2, (m % 2) * 192 : (m % 2) * 192 + 192, :] = value.astype(BF16)

    fill(
        look,
        jnp.where(dest >= 0, (dest % 4) * CAP + rank, -1),
        lambda f: jnp.where(field(0, f) == 1, field(1, f) // 4, -1),
        store,
    )


def bucket_plain(fields, table, qr_ref, lab_ref, look):
    field_t, col = fields_of(fields)

    def field(t, f):
        return col[:, t * F + f : t * F + f + 1]

    shard, row, at = 3 + 2 * table, 4 + 2 * table, 64 * table
    dest = jnp.where(field_t[0] == 0, field_t[shard], -1)
    rank_t, hits = ranks_of(dest, NDEV, ramp_of())
    rank_col = as_columns(rank_t)
    lane = iota((SAMP, 128), 1)
    parts = []
    for f in range(F):
        mark = field(row, f) + 1
        rank = rank_col[:, f : f + 1]
        value = jnp.where(lane < at + 32, mark // 64, mark % 64)
        hit = ((lane - at == rank) | (lane - at - 32 == rank)) & (field(0, f) == 0)
        parts.append(jnp.where(hit, value, 0).astype(F32).astype(BF16))
    lab = jnp.dot(jnp.concatenate(hits, axis=1), jnp.concatenate(parts, axis=0), preferred_element_type=F32)
    lab = lab.reshape(lab_ref.shape)
    lab_ref[...] = lab if table == 0 else lab_ref[...] + lab

    def store(m, h, value):
        qr_ref[h * 64 + m * 8 : h * 64 + m * 8 + 8, table] = value.reshape(8, QCAP, E).astype(BF16)

    fill(
        look,
        jnp.where(dest >= 0, (dest % 64) * QCAP + rank_t.astype(jnp.int32), -1),
        lambda f: jnp.where(field(0, f) == 0, field(shard, f) // 64, -1),
        store,
    )


def flat_marks(lab):
    slot = iota((128, 1536), 1)
    inner = slot % 384
    spread = onehot(iota((128, 1536), 0) == (slot // 384) * 32 + inner % QCAP)
    wide = jnp.dot(lab.astype(BF16), spread, preferred_element_type=F32)
    wide = jnp.where(inner // QCAP == iota((128, 1536), 0) % 16, wide, 0.0).astype(BF16)
    gather = onehot(iota((16, 128), 0) == iota((16, 128), 1) // 16)
    flat = jnp.dot(gather, wide, preferred_element_type=F32)[:8]
    return [flat[:, t * 768 : t * 768 + 384] * 64.0 + flat[:, t * 768 + 384 : t * 768 + 768] for t in range(2)]


def sum_rows(marks, group, block, n_rows, put):
    hi_rows = n_rows // 4
    mark = marks.astype(jnp.int32) - 1
    low = jnp.where(mark >= 0, mark // hi_rows, -1)
    high = jnp.where(mark >= 0, mark % hi_rows, -1)
    low_col = jnp.transpose(
        jnp.concatenate([low.astype(F32), jnp.zeros((SAMP - 24, SAMP), F32)], axis=0)
    ).astype(jnp.int32)
    order = [group(i, j) for i in range(8) for j in range(3)]
    rhs = []
    for i in range(8):
        values = block(i)
        for j in range(3):
            g = group(i, j)
            v = values[j * 128 : (j + 1) * 128]
            which = low_col[:, g : g + 1]
            rhs.append(jnp.concatenate([jnp.where(which == k, v, 0.0).astype(BF16) for k in range(4)], axis=1))
    rhs = jnp.concatenate(rhs, axis=0)
    for m in range(hi_rows // 256):
        want = iota((256, SAMP), 0) + m * 256
        picked = jnp.concatenate([onehot(want == high[g : g + 1, :]) for g in order], axis=1)
        out = jnp.dot(picked, rhs, preferred_element_type=F32)
        for k in range(4):
            put(k * hi_rows + m * 256, out[:, k * E : (k + 1) * E])


MESH = pl.DeviceIdType.MESH
STREAMS = ((3072, 0, (1, 2, 0)), (3072, 3072, (2, 0, 1)), (2048, 6144, (0, 1, 2)))


def piece(stream, stage):
    return STREAMS[stream][0] // 4 ** (stage + 1)


def stage_rows():
    table, at = {}, 0
    for stage in range(3):
        for stream in range(3):
            table[stage, stream] = at
            at += 3 * piece(stream, stage)
    return table, at


ROWS_AT, ROWS_ALL = stage_rows()
GAPS = (0, 46, 36, 0, 28, 17, 0, 0, 0, 0)


def step_kernel(
    feat_hbm, w_hbm, b_hbm, g_hbm, h0, h1, h2, h3, h4, h5, h6,
    full_ref, bout_ref, agrad_ref, q_ref, r_ref,
    feat_ref, w_ref, b_ref, g_ref, f0, f1, f2, f3, f4, f5, f6, in_sem,
    feat_in, dpre_ref, dpre_in, data, look, sbuf, rbuf, bsum,
    qr_ref, qr_in, qlab_ref, qlab_in, adm_ref, adm_in, alab_ref, alab_in, osum, osum_in,
    pair_sem, rs_sem, ag_sem, fw_sem, b_sem, adm_sem, qr_sem, tab_sem,
):
    dp, tab = lax.axis_index("dp"), lax.axis_index("table")
    core, x = lax.rem(dp, 2), lax.div(dp, 2)
    y, z = lax.div(tab, 4), lax.rem(tab, 4)
    me = dp * 16 + tab
    place = (x, y, z)

    def turn(value, step):
        return lax.rem(value + step + 4, 4)

    def beside(axis, step):
        if axis == 0:
            return (turn(x, step) * 2 + core, tab)
        if axis == 1:
            return (dp, turn(y, step) * 4 + z)
        return (dp, y * 4 + turn(z, step))

    partner = (dp + 1 - 2 * core, tab)

    def remote(src, dst, sems, device):
        return pltpu.make_async_remote_copy(
            src_ref=src, dst_ref=dst, send_sem=sems[0], recv_sem=sems[1], device_id=device, device_id_type=MESH
        )

    def sems(array, *at):
        return array.at[(0,) + at], array.at[(1,) + at]

    def load(i, src, dst):
        copy = pltpu.make_async_copy(src, dst, in_sem.at[i])
        copy.start()
        return copy

    feat_load = load(0, feat_hbm, feat_ref)
    w_loads = [load(1 + i, w_hbm.at[pl.ds(i * 512, 512)], w_ref.at[pl.ds(i * 512, 512)]) for i in range(4)]
    late_loads = [load(5, b_hbm, b_ref), load(6, g_hbm, g_ref)]
    held = (h0, h1, h2, h3, h4, h5, h6)
    fields = (f0, f1, f2, f3, f4, f5, f6)
    field_loads = [load(7 + i, held[i], fields[i]) for i in range(7)]

    barrier = pltpu.get_barrier_semaphore()

    @pl.loop(1, NDEV)
    def _(i):
        peer = lax.rem(me + i, NDEV)
        pl.semaphore_signal(
            barrier, inc=1, device_id=(lax.div(peer, 16), lax.rem(peer, 16)), device_id_type=MESH
        )

    feat_load.wait()
    pre = jnp.zeros((SAMP, HID), F32)
    for i in range(4):
        w_loads[i].wait()
        pre = pre + jnp.dot(
            feat_ref[:, i * 512 : i * 512 + 512], w_ref[i * 512 : i * 512 + 512, :], preferred_element_type=F32
        )
    for copy in late_loads:
        copy.wait()
    pre = pre + b_ref[...]
    sig = 1.0 / (1.0 + jnp.exp(-pre))
    dpre_ref[...] = (g_ref[...].astype(F32) * sig * (1.0 + pre * (1.0 - sig))).astype(BF16)
    pl.semaphore_wait(barrier, NDEV - 1)

    def start_adm():
        for i in range(1, NOWN):
            peer = lax.rem(dp + i, NOWN)
            remote(adm_ref.at[peer], adm_in.at[dp], sems(adm_sem, 0), (peer, tab)).start()
            remote(alab_ref.at[peer], alab_in.at[dp], sems(adm_sem, 1), (peer, tab)).start()
        adm_in[dp] = adm_ref[dp]
        alab_in[dp] = alab_ref[dp]

    def wait_all(src, dst, array, at):
        pltpu.make_async_copy(src, src, array.at[(0,) + at]).wait()
        pltpu.make_async_copy(dst, dst, array.at[(1,) + at]).wait()

    def sum_adm():
        wait_all(adm_ref.at[0:7], adm_in.at[0:7], adm_sem, (0,))
        wait_all(alab_ref.at[0:7], alab_in.at[0:7], adm_sem, (1,))

        def put(at, value):
            for j in range(2):
                osum[at // 128 + j] = value[j * 128 : j * 128 + 128].astype(BF16)

        marks = jnp.concatenate([alab_in[o] for o in range(NOWN)], axis=0)
        sum_rows(marks, lambda i, j: i * 3 + j, lambda i: adm_in[i].astype(F32), OWN_ROWS, put)

        @pl.loop(1, 16)
        def _(i):
            peer = lax.rem(tab + i * 7, 16)
            remote(osum.at[peer], osum_in.at[tab], sems(tab_sem), (dp, peer)).start()

        osum_in[tab] = osum[tab]

    def finish_adm():
        wait_all(osum.at[0:15], osum_in.at[0:15], tab_sem, ())
        total = osum_in[0].astype(F32)
        for j in range(1, 16):
            total = total + osum_in[j].astype(F32)
        agrad_ref[...] = total

    def start_qr(first, count):
        @pl.loop(first, first + count)
        def _(i):
            peer = lax.rem(me + i * 37, NDEV)
            device = (lax.div(peer, 16), lax.rem(peer, 16))
            remote(qr_ref.at[peer], qr_in.at[me], sems(qr_sem, 0), device).start()
            remote(qlab_ref.at[peer], qlab_in.at[me], sems(qr_sem, 1), device).start()

    sent = [1]

    def gap(k):
        for work in before.get(k, ()):
            work()
        if GAPS[k]:
            start_qr(sent[0], GAPS[k])
            sent[0] += GAPS[k]
        for work in after.get(k, ()):
            work()

    bias_slots = ((0, 4, x), (4, 4, y), (8, 4, z))

    def bias_start(k):
        first, count, mine = bias_slots[k]
        slot = first + mine
        for i in range(1, count):
            device = beside(k, i)
            remote(bsum.at[slot], bsum.at[slot], sems(b_sem, first + i), device).start()

    def bias_wait(k):
        first, count, mine = bias_slots[k]
        for i in range(1, count):
            pltpu.make_async_copy(bsum.at[first], bsum.at[first], b_sem.at[0, first + i]).wait()
            pltpu.make_async_copy(bsum.at[first], bsum.at[first], b_sem.at[1, first + i]).wait()
        total = bsum[first]
        for i in range(1, count):
            total = total + bsum[first + i]
        return total

    theirs = pl.ds(pl.multiple_of((1 - core) * HALF, 128), HALF)
    pair = [
        remote(feat_ref.at[:, theirs], feat_in, sems(pair_sem, 0), partner),
        remote(dpre_ref, dpre_in, sems(pair_sem, 1), partner),
    ]
    for copy in pair:
        copy.start()
    for i in range(F // 2):
        part = lax.dot_general(
            dpre_ref[...], w_ref[i * 256 : (i + 1) * 256, :], (((1,), (1,)), ((), ())), preferred_element_type=F32
        )
        look[2 * i] = part[:, :E]
        look[2 * i + 1] = part[:, E:]
    for copy in pair:
        copy.wait()
    both = jnp.concatenate([dpre_ref[...], dpre_in[...]], axis=0)
    bias = jnp.sum(dpre_ref[...].astype(F32), axis=0, keepdims=True) + jnp.sum(
        dpre_in[...].astype(F32), axis=0, keepdims=True
    )
    bsum[x] = jnp.concatenate([bias[:, k * 128 : k * 128 + 128] for k in range(HID // 128)], axis=0)

    def make_adm():
        for copy in field_loads:
            copy.wait()
        bucket_adm(fields, adm_ref, alab_ref, look)
        start_adm()

    def make_q():
        bucket_plain(fields, 0, qr_ref, qlab_ref, look)

    def make_r():
        bucket_plain(fields, 1, qr_ref, qlab_ref, look)
        qr_in[me] = qr_ref[me]
        qlab_in[me] = qlab_ref[me]

    def sum_plain(t, out_ref):
        def put(at, value):
            out_ref[at : at + 256, :] = value

        marks = flat_marks(qlab_in[:, 0, :])[t]
        sum_rows(
            jnp.concatenate([marks[:, j * 128 : j * 128 + 128] for j in range(3)], axis=0),
            lambda i, j: j * 8 + i,
            lambda i: qr_in[i * 16 : i * 16 + 16, t].astype(F32).reshape(384, E),
            QROWS_DEV,
            put,
        )

    def sum_q():
        wait_all(qr_ref.at[0 : NDEV - 1], qr_in.at[0 : NDEV - 1], qr_sem, (0,))
        wait_all(qlab_ref.at[0 : NDEV - 1], qlab_in.at[0 : NDEV - 1], qr_sem, (1,))
        sum_plain(0, q_ref)

    def sum_r():
        sum_plain(1, r_ref)

    def half_block(k):
        rows, first, _ = STREAMS[k]
        col, width = first // HALF * 128, rows // HALF * 128
        for i in range(HALF // 256):
            at = pl.multiple_of(core * HALF + i * 256, 256)
            feats = jnp.concatenate([feat_ref[:, pl.ds(at, 256)], feat_in[:, i * 256 : i * 256 + 256]], axis=0)
            block = lax.dot_general(
                feats, both[:, col : col + width], (((0,), (0,)), ((), ())), preferred_element_type=F32
            )
            for j in range(width // 128):
                to = first + j * HALF + i * 256
                data[to : to + 256, :] = block[:, j * 128 : j * 128 + 128]

    first_row = [pl.multiple_of(jnp.int32(0) + STREAMS[k][1], 16) for k in range(3)]
    starts = [[], [], []]
    flying = [[], [], []]

    def send(k, *copy):
        flying[k].append(remote(*copy))
        flying[k][-1].start()

    def land(k):
        for copy in flying[k]:
            copy.wait()
        flying[k] = []

    def where_at(k, stage):
        axis = STREAMS[k][2][stage]
        return piece(k, stage), axis, place[axis], ROWS_AT[stage, k]

    def reduce_far(stage, k):
        n, axis, p, at = where_at(k, stage)
        h, cur = n // 2, first_row[k]
        sbuf[at : at + n, :] = data[pl.ds(pl.multiple_of(cur + turn(p, 2) * n, 16), n), :].astype(BF16)
        for d, step in ((0, 1), (1, -1)):
            part = slice(at + d * h, at + d * h + h)
            send(k, sbuf.at[part], rbuf.at[part], sems(rs_sem, stage, k, d), beside(axis, step))

    def reduce_near(stage, k):
        n, axis, p, at = where_at(k, stage)
        h, cur = n // 2, first_row[k]
        land(k)
        for d, step in ((0, 1), (1, -1)):
            row = pl.multiple_of(cur + turn(p, step) * n, 16)
            to = at + n + d * n
            for e in range(2):
                value = data[pl.ds(row + e * h, h), :]
                if e == d:
                    value = value + rbuf[at + d * h : at + d * h + h, :].astype(F32)
                sbuf[to + e * h : to + e * h + h, :] = value.astype(BF16)
            part = slice(to, to + n)
            send(k, sbuf.at[part], rbuf.at[part], sems(rs_sem, stage, k, 2 + d), beside(axis, step))

    def reduce_end(stage, k):
        n, axis, p, at = where_at(k, stage)
        cur = first_row[k]
        land(k)
        mine = pl.multiple_of(cur + p * n, 16)
        value = data[pl.ds(mine, n), :]
        for i in range(1 - stage, 3):
            value = value + rbuf[at + i * n : at + i * n + n, :].astype(F32)
        data[pl.ds(mine, n), :] = value
        starts[k].append(cur)
        first_row[k] = mine

    def direct_send(stage, k):
        n, axis, p, at = where_at(k, stage)
        for i in range(1, 4):
            part = slice(at + (i - 1) * n, at + i * n)
            row = pl.multiple_of(first_row[k] + turn(p, i) * n, 16)
            sbuf[part, :] = data[pl.ds(row, n), :].astype(BF16)
            send(k, sbuf.at[part], rbuf.at[part], sems(rs_sem, stage, k, i - 1), beside(axis, i))

    def last_end(k):
        n, axis, p, at = where_at(k, 2)
        land(k)
        rows = pl.ds(pl.multiple_of(first_row[k] + p * n, 16), n)
        value = data[rows, :]
        for i in range(3):
            value = value + rbuf[at + i * n : at + i * n + n, :].astype(F32)
        full_ref[core, rows, :] = value.astype(BF16)
        for i in range(1, 4):
            spread(k, rows, sems(ag_sem, 2, k, i - 1), beside(axis, i))

    def spread(k, rows, pair_of, device):
        send(k, full_ref.at[core, rows], full_ref.at[core, rows], pair_of, device)

    def gather_near(stage, k):
        n, axis, p, _ = where_at(k, stage)
        land(k)
        rows = pl.ds(pl.multiple_of(starts[k][stage] + p * n, 16), n)
        for d, step in ((0, 1), (1, -1)):
            spread(k, rows, sems(ag_sem, stage, k, d), beside(axis, step))

    def gather_far(stage, k):
        n, axis, p, _ = where_at(k, stage)
        h = n // 2
        land(k)
        for d, step in ((0, 1), (1, -1)):
            rows = pl.ds(pl.multiple_of(starts[k][stage] + turn(p, -step) * n + d * h, 8), h)
            spread(k, rows, sems(ag_sem, stage, k, 2 + d), beside(axis, step))

    forwards = []

    def forward(k, which, step):
        n, _, p, _ = where_at(k, 0)
        rows = pl.ds(pl.multiple_of(starts[k][0] + turn(p, step) * n, 16), n)
        forwards.append(
            remote(full_ref.at[core, rows], full_ref.at[core, rows], sems(fw_sem, k, which), partner)
        )
        forwards[-1].start()

    def bias_turn(stage):
        total = bias_wait(stage)
        if stage == 2:
            bout_ref[...] = total
        else:
            first, _, mine = bias_slots[stage + 1]
            bsum[first + mine] = total
            bias_start(stage + 1)

    before = {0: (make_adm,), 1: (make_q, make_r)}
    after = {4: (sum_adm,), 6: (finish_adm,), 8: (sum_q,), 9: (sum_r,)}

    bias_start(0)
    for k in range(3):
        half_block(k)
        reduce_far(0, k)
    gap(0)
    for k in range(3):
        reduce_near(0, k)
    gap(1)
    for k in range(3):
        reduce_end(0, k)
        direct_send(1, k)
    bias_turn(0)
    gap(2)
    for k in range(3):
        reduce_end(1, k)
        direct_send(2, k)
    bias_turn(1)
    gap(4)
    for k in range(3):
        last_end(k)
    bias_turn(2)
    gap(5)
    for k in range(3):
        n, axis, p, _ = where_at(k, 1)
        land(k)
        for i in range(1, 4):
            rows = pl.ds(pl.multiple_of(starts[k][1] + p * n, 16), n)
            spread(k, rows, sems(ag_sem, 1, k, i - 1), beside(axis, i))
    gap(6)
    for k in range(3):
        gather_near(0, k)
        forward(k, 0, 0)
    gap(8)
    for k in range(3):
        gather_far(0, k)
        forward(k, 1, 1)
        forward(k, 2, -1)
    gap(9)
    for k in range(3):
        land(k)
        forward(k, 3, 2)
    for copy in forwards:
        copy.wait()


def finish_kernel(full_ref, q_ref, r_ref, a_ref, b_ref, w_out, q_out, r_out, a_out, b_out, wide, sem):
    stores = []

    def store(src, dst):
        stores.append(pltpu.make_async_copy(src, dst, sem.at[len(stores)]))
        stores[-1].start()

    store(q_ref, q_out)
    store(r_ref, r_out)
    for i in range(8):
        for k in range(HID // 128):
            value = full_ref[i // 4, k, i % 4 * 256 : i % 4 * 256 + 256, :]
            wide[i * 256 : i * 256 + 256, k * 128 : k * 128 + 128] = value.astype(F32)
        store(wide.at[i * 256 : i * 256 + 256], w_out.at[i * 256 : i * 256 + 256])
    store(a_ref, a_out)
    store(b_ref, b_out)
    for copy in stores:
        copy.wait()


def spec():
    return pl.BlockSpec(memory_space=VMEM)


def shape(dims, dtype):
    return jax.ShapeDtypeStruct(dims, dtype)


def local(features, w_first, b_first, grad_out, admit, owner, adm_row, q_shard, q_local, r_shard, r_local):
    fields = [
        f.T if f.ndim == 2 else f.transpose(1, 2, 0)
        for f in (admit, owner, adm_row, q_shard, q_local, r_shard, r_local)
    ]
    dma = pltpu.SemaphoreType.DMA
    full, b_rows, a_rows, q_rows, r_rows = pl.pallas_call(
        step_kernel,
        out_shape=(
            shape((2, HALF_ROWS, 128), BF16),
            shape((8, 128), F32),
            shape((128, E), F32),
            shape((QROWS_DEV, E), F32),
            shape((QROWS_DEV, E), F32),
        ),
        in_specs=[pl.BlockSpec(memory_space=pltpu.HBM)] * 11,
        out_specs=tuple([spec()] * 5),
        scratch_shapes=[
            VMEM((SAMP, WROWS), BF16),
            VMEM((WROWS, HID), BF16),
            VMEM((1, HID), F32),
            VMEM((SAMP, HID), BF16),
            *[VMEM(f.shape, jnp.int32) for f in fields],
            dma((14,)),
            VMEM((SAMP, HALF), BF16),
            VMEM((SAMP, HID), BF16),
            VMEM((SAMP, HID), BF16),
            VMEM((HALF_ROWS, 128), F32),
            VMEM((F, SAMP, E), F32),
            VMEM((ROWS_ALL, 128), BF16),
            VMEM((ROWS_ALL, 128), BF16),
            VMEM((12, 8, 128), F32),
            VMEM((NDEV, 2, QCAP, E), BF16),
            VMEM((NDEV, 2, QCAP, E), BF16),
            VMEM((NDEV, 1, 128), F32),
            VMEM((NDEV, 1, 128), F32),
            VMEM((NOWN, CAP, E), BF16),
            VMEM((NOWN, CAP, E), BF16),
            VMEM((NOWN, 3, 128), F32),
            VMEM((NOWN, 3, 128), F32),
            VMEM((16, 128, E), BF16),
            VMEM((16, 128, E), BF16),
            dma((2, 2)),
            dma((2, 3, 3, 4)),
            dma((2, 3, 3, 4)),
            dma((2, 3, 4)),
            dma((2, 12)),
            dma((2, 2)),
            dma((2, 2)),
            dma((2,)),
        ],
        compiler_params=pltpu.CompilerParams(vmem_limit_bytes=44 << 20, collective_id=0, has_side_effects=True),
        name="step",
    )(*[pltpu.with_memory_space_constraint(v, pltpu.HBM) for v in (features, w_first, b_first.reshape(1, HID), grad_out, *fields)])
    w_grad, q_grad, r_grad, adm_grad, b_sum = pl.pallas_call(
        finish_kernel,
        out_shape=(
            shape((WROWS, HID), F32),
            shape((QROWS_DEV, E), F32),
            shape((QROWS_DEV, E), F32),
            shape((128, E), F32),
            shape((8, 128), F32),
        ),
        in_specs=[spec()] * 5,
        out_specs=tuple([pl.BlockSpec(memory_space=pltpu.HBM)] * 5),
        scratch_shapes=[VMEM((WROWS, HID), F32), dma((12,))],
        compiler_params=pltpu.CompilerParams(vmem_limit_bytes=20 << 20),
        name="finish",
    )(full.reshape(2, 8, HALF, 128), q_rows, r_rows, a_rows, b_rows)
    return (w_grad, b_sum.reshape(HID), adm_grad, q_grad, r_grad)


def solution(mesh):
    both = ("dp", "table")
    two, three = P(both, None), P(both, None, None)
    return jax.shard_map(
        local,
        mesh=mesh,
        in_specs=(two, P(), P(), two, two, three, two, three, two, three, two),
        out_specs=(P(), P(), two, two, two),
        check_vma=False,
    )
```
